128 devices in a mesh: expert: 16 (over y, x_lo, core), tensor: 8 (over x_hi, z).
Axes of the slice: x: 4 (x_hi: 2, x_lo: 2; x = x_hi * 2 + x_lo), y: 4, z: 4, core: 2. Of those that a mesh axis runs over, the one named last changes fastest.
Arguments:
- tokens: bfloat16 [4096, 7168], P(('expert', 'tensor')), may hold values from -6 to 6
- expert_ids: int32 [4096, 2], P('expert'), may hold values from 0 to 2, all different within a row
- gate_scores: int32 [4096, 2], P('expert'), may hold values from 1 to 64
- gate_weight: bfloat16 [3, 7168, 2048], P(None, ('expert', 'tensor')), may hold values from -0.0625 to 0.0625
- up_weight: bfloat16 [3, 7168, 2048], P(None, ('expert', 'tensor')), may hold values from -0.0625 to 0.0625
- down_weight: bfloat16 [3, 7168, 2048], P(None, ('expert', 'tensor')), may hold values from -0.1875 to 0.1875
Outputs:
- mixed: bfloat16 [4096, 7168], P(('expert', 'tensor'))
The draws below stay inside these ranges and needn't reach their ends.
Inputs may be any that keep to these rules, and one draw needn't show every extreme that they name: `expert_ids`: each row names 2 different experts.
All inputs are finite; a program needn't handle non-finite values.
Results may differ from the reference program's by a relative error of at most 0.015.
Values may be sent and summed in bfloat16 or wider, within the bound.
A program may use at most 128 MiB of HBM per device.

```python
import jax
import jax.numpy as jnp
from jax import lax

D = 7168
FF = 2048
EXPERTS = 3
TOP = 2
TOKENS = 4096
N_TENSOR = 8


def plant(entries, stream_key, least, high):
    dims = entries.shape
    place = [jax.random.randint(jax.random.fold_in(stream_key, axis), (), 0, dims[axis]) for axis in range(len(dims))]
    entries = entries.at[tuple(place)].set(least)
    longest = dims.index(max(dims))
    place[longest] = (place[longest] + 1) % dims[longest]
    return entries.at[tuple(place)].set(high)


def block_scale(own_key, extent, split, smallest, largest):
    gain = 1.0
    for dim, parts in split:
        heights = jax.random.uniform(jax.random.fold_in(jax.random.fold_in(own_key, 6), dim), (parts,), jnp.float32, smallest / len(split), largest / len(split))
        gain = gain * jnp.repeat(jnp.exp(heights), extent[dim] // parts).reshape((-1,) + (1,) * (len(extent) - 1 - dim))
    return gain


def different_ones(stream_key, rows, amount, top, lift):
    ranking = jax.random.permutation(jax.random.fold_in(stream_key, 1), amount)
    favour = ranking
    for power in range(3):
        favour = favour * favour // amount
    favour = favour * lift // amount
    chance = jax.random.randint(jax.random.fold_in(stream_key, 2), (rows, amount), 0, 4096) + favour
    holders = jax.random.permutation(jax.random.fold_in(stream_key, 3), rows)[jnp.arange(amount) % rows]
    chance = jnp.where(jnp.arange(rows)[:, None] == holders[None, :], 1 << 14, chance)
    score = chance * amount + jnp.arange(amount)
    return lax.top_k(score.astype(jnp.int32), top)[1].astype(jnp.int32)


def scatter_about(stream_key, shape, deviation, most, cuts=(), kind=jnp.bfloat16):
    gain = block_scale(stream_key, shape, cuts, -0.22, 0.18) if cuts else 1.0
    values = jax.random.normal(stream_key, shape, jnp.float32) * deviation * gain
    return jnp.minimum(jnp.maximum(values, -most), most).astype(kind)


def setup_inputs(seed: int = 0) -> dict:
    keys = jax.random.split(jax.random.key(seed), 7)
    tokens = scatter_about(keys[0], (TOKENS, D), 1.0, 6.0, ((0, 128),))
    expert_ids = different_ones(keys[1], TOKENS, EXPERTS, TOP, 0)
    gate_scores = plant(jax.random.randint(keys[2], (TOKENS, TOP), 1, 65), jax.random.fold_in(keys[2], 1), 1, 64).astype(jnp.int32)
    gate_weight = scatter_about(keys[3], (EXPERTS, D, FF), D ** -0.5, 0.0625, ((1, 128),))
    up_weight = scatter_about(keys[4], (EXPERTS, D, FF), D ** -0.5, 0.0625, ((1, 128),))
    down_weight = scatter_about(keys[5], (EXPERTS, D, FF), (FF // 2) ** -0.5, 0.1875, ((1, 128),))
    return {"tokens": tokens, "expert_ids": expert_ids, "gate_scores": gate_scores, "gate_weight": gate_weight, "up_weight": up_weight, "down_weight": down_weight}


def activate(gate_sum, up_sum, weight_col):
    return (jax.nn.silu(gate_sum) * up_sum * weight_col).astype(jnp.bfloat16)


def reference(tokens, expert_ids, gate_scores, gate_weight, up_weight, down_weight):
    scores = gate_scores.astype(jnp.float32)
    score_sum = jnp.sum(scores, axis=1, keepdims=True)
    labels = jnp.arange(EXPERTS, dtype=jnp.int32)
    picked = (expert_ids[:, :, None] == labels[None, None, :]).astype(jnp.float32)
    combine = jnp.sum(scores[:, :, None] * picked, axis=1) / score_sum
    hiddens = []
    for which in range(EXPERTS):
        gate_sum = jnp.dot(tokens, gate_weight[which], preferred_element_type=jnp.float32)
        up_sum = jnp.dot(tokens, up_weight[which], preferred_element_type=jnp.float32)
        hiddens.append(activate(gate_sum, up_sum, combine[:, which:which + 1]))
    width = FF // N_TENSOR
    result = jnp.zeros((TOKENS, D), jnp.float32)
    for shard in range(N_TENSOR):
        partial_sum = jnp.zeros((TOKENS, D), jnp.float32)
        for which in range(EXPERTS):
            hid_block = hiddens[which][:, shard * width:(shard + 1) * width]
            down_block = down_weight[which][:, shard * width:(shard + 1) * width]
            partial_sum = partial_sum + lax.dot_general(hid_block, down_block, (((1,), (1,)), ((), ())), preferred_element_type=jnp.float32)
        rounded = lax.optimization_barrier(partial_sum.astype(jnp.bfloat16))
        result = result + rounded.astype(jnp.float32)
    return result.astype(jnp.bfloat16)
```

```python
import jax
import jax.numpy as jnp
from jax import lax
from jax.experimental import pallas as pl
from jax.experimental.pallas import tpu as pltpu
from jax.sharding import PartitionSpec as P

MESH = pl.DeviceIdType.MESH
F32 = jnp.float32
BF16 = jnp.bfloat16

N = 4
EXPERTS = 3
D = 7168
ROWS = 32
DEPTH = 56
CHUNK = 448
QUARTER = 1792
UNITS = 128
HALF = D // 2
PIECES = 8
WIDE = D // PIECES

PLANE = (
    (1, 0), (3, 0), (0, 1), (0, 3), (2, 0), (0, 2), (1, 1), (3, 3),
    (2, 1), (1, 3), (3, 1), (2, 3), (1, 2), (3, 2), (2, 2),
)


def place():
    e = lax.axis_index("expert")
    t = lax.axis_index("tensor")
    y, xl, c = lax.div(e, 4), lax.rem(lax.div(e, 2), 2), lax.rem(e, 2)
    xh, z = lax.div(t, 4), lax.rem(t, 4)
    return e, t, y, xh * 2 + xl, z, c, xl, xh


def device(y, x, z, c):
    return {
        "expert": y * 4 + lax.rem(x, 2) * 2 + c,
        "tensor": lax.div(x, 2) * 4 + z,
    }


def ring(v, d):
    return lax.rem(v + d, N)


def kernel(
    tok, ids, scores, gate, up, down, out,
    xs, ws, acc, hid, part, r1, s1, r2, comb,
    ssem, asend, arecv, wrecv, trecv, crecv, rrecv1, rrecv2, lsem,
):
    e, t, y, x, z, c, xl, xh = place()
    mine = e * 8 + t
    sends = []

    def send(src, dst, recv, to):
        cp = pltpu.make_async_remote_copy(
            src_ref=src,
            dst_ref=dst,
            send_sem=ssem.at[len(sends)],
            recv_sem=recv,
            device_id=to,
            device_id_type=MESH,
        )
        cp.start()
        sends.append(cp)

    def arrived(ref, sem):
        pltpu.make_async_copy(ref, ref, sem).wait()

    which = lax.broadcasted_iota(jnp.int32, (8, 256), 0)
    marks = scores[...].astype(F32)
    first, second = marks[0:1, :], marks[1:2, :]
    picked = jnp.where(ids[0:1, :] == which, first, 0.0) + jnp.where(
        ids[1:2, :] == which, second, 0.0
    )
    comb[xl] = picked / (first + second)

    barrier = pltpu.get_barrier_semaphore()
    peers = [device(y, ring(x, dx), ring(z, dz), c) for dx, dz in PLANE]
    north, south = device(ring(y, 1), x, z, c), device(ring(y, 3), x, z, c)
    partner = device(y, x, z, 1 - c)
    for to in [*peers, north, south, partner]:
        pl.semaphore_signal(barrier, inc=1, device_id=to, device_id_type=MESH)
    pl.semaphore_wait(barrier, len(peers) + 3)

    own_rows = pl.ds(pl.multiple_of(mine * DEPTH, 8), DEPTH)

    def columns(px, pz):
        return pl.ds(pl.multiple_of((px * N + pz) * UNITS, UNITS), UNITS)

    def spread(ref, lo, kind):
        for (dx, dz), to in zip(PLANE, peers):
            cols = columns(ring(x, dx), ring(z, dz))
            pltpu.make_async_remote_copy(
                src_ref=ref.at[:, :, cols],
                dst_ref=ws.at[lo : lo + EXPERTS, own_rows, :],
                send_sem=asend.at[kind],
                recv_sem=arecv.at[kind, xl],
                device_id=to,
                device_id_type=MESH,
            ).start()

    def keep(ref, lo, kind):
        pltpu.make_async_copy(
            ref.at[:, :, columns(x, z)],
            ws.at[lo : lo + EXPERTS, own_rows, :],
            arecv.at[kind, xl],
        ).start()

    h0, h1 = pl.ds(0, HALF), pl.ds(HALF, HALF)
    own_tok = pltpu.make_async_copy(tok, xs.at[x, z], lsem)
    own_tok.start()
    keep(gate, 0, 0)
    keep(up, 3, 0)
    keep(down, 6, 1)
    spread(gate, 0, 0)
    spread(up, 3, 0)
    other = device(y, xh * 2 + 1 - xl, z, c)
    send(comb.at[xl], comb.at[xl], crecv, other)

    def along(axis, d):
        if axis == 0:
            return device(y, ring(x, d), z, c)
        return device(y, x, ring(z, d), c)

    def send_tokens(src, bx, bz, half, axis):
        cols = (h0, h1)[half]
        for d in (1, 3, 2):
            send(src, xs.at[bx, bz, :, cols], trecv.at[half, bx, bz], along(axis, d))

    send_tokens(tok.at[:, h0], x, z, 0, 0)
    send_tokens(tok.at[:, h1], x, z, 1, 1)
    send_tokens(tok.at[:, h0], x, z, 0, 1)
    send_tokens(tok.at[:, h1], x, z, 1, 0)
    spread(down, 6, 1)

    bounds = ((0, 6), (6, 9))

    def chunk(kind, cy, cx, cc):
        lo, hi = bounds[kind]
        k = cy * 4 + cx * 2 + cc
        rows = pl.ds(pl.multiple_of(k * CHUNK, CHUNK), CHUNK)
        return ws.at[lo:hi, rows, :], wrecv.at[kind, k]

    def pass_on(kind, cy, cx, to):
        ref, sem = chunk(kind, cy, cx, c)
        send(ref, ref, sem, to)

    def wait_chunk(kind, cy, cx, cc):
        ref, sem = chunk(kind, cy, cx, cc)
        arrived(ref, sem)

    def own_chunks(kind):
        arrived(chunk(kind, y, 0, c)[0], arecv.at[kind, 0])
        pass_on(kind, y, 0, north)
        pass_on(kind, y, 0, partner)
        arrived(chunk(kind, y, 1, c)[0], arecv.at[kind, 1])
        pass_on(kind, y, 1, south)
        pass_on(kind, y, 1, north)
        pass_on(kind, y, 0, south)
        pass_on(kind, y, 1, partner)

    before, after, across = ring(y, 3), ring(y, 1), ring(y, 2)

    def relay(kind):
        wait_chunk(kind, before, 0, c)
        pass_on(kind, before, 0, north)
        pass_on(kind, before, 0, partner)
        wait_chunk(kind, after, 1, c)
        pass_on(kind, after, 1, south)
        pass_on(kind, after, 1, partner)

    def hand_over(kind):
        wait_chunk(kind, before, 1, c)
        pass_on(kind, before, 1, partner)
        wait_chunk(kind, after, 0, c)
        pass_on(kind, after, 0, partner)

    def hand_over_far(kind):
        for cx in range(2):
            wait_chunk(kind, across, cx, c)
            pass_on(kind, across, cx, partner)

    def from_partner(kind, cy):
        for cx in range(2):
            wait_chunk(kind, cy, cx, 1 - c)

    def wait_tokens(bx, bz, half):
        arrived(xs.at[bx, bz, :, (h0, h1)[half]], trecv.at[half, bx, bz])

    own_chunks(0)
    for d in (3, 1, 2):
        bx = ring(x, d)
        wait_tokens(bx, z, 0)
        send_tokens(xs.at[bx, z, :, h0], bx, z, 0, 1)
        bz = ring(z, d)
        wait_tokens(x, bz, 1)
        send_tokens(xs.at[x, bz, :, h1], x, bz, 1, 0)
    relay(0)
    own_chunks(1)
    hand_over(0)
    own_tok.wait()
    for bd in range(1, N):
        for ad in range(N):
            wait_tokens(ring(x, ad), ring(z, bd), 0)
            wait_tokens(ring(x, bd), ring(z, ad), 1)

    def products(cy, start):
        span = pl.ds(pl.multiple_of(cy * QUARTER, 256), QUARTER)

        def one(w, carry):
            left = xs[:, :, :, span].reshape(N * N * ROWS, QUARTER)
            right = jnp.concatenate([ws[w, span, :], ws[EXPERTS + w, span, :]], axis=1)
            total = jnp.dot(left, right, preferred_element_type=F32)
            acc[w] = total if start else acc[w] + total
            return carry

        lax.fori_loop(0, EXPERTS, one, 0)

    from_partner(0, y)
    products(y, True)
    from_partner(0, before)
    products(before, False)
    from_partner(0, after)
    products(after, False)
    relay(1)
    hand_over_far(0)
    hand_over(1)
    from_partner(0, across)
    products(across, False)

    arrived(comb.at[1 - xl], crecv)
    for bx in range(N):
        column = comb[bx % 2][:, (bx // 2) * 128 : (bx // 2) * 128 + 128].T
        rows = slice(bx * N * ROWS, (bx + 1) * N * ROWS)
        for w in range(EXPERTS):
            g = acc[w, rows, 0:UNITS]
            u = acc[w, rows, UNITS : 2 * UNITS]
            value = g / (1.0 + jnp.exp(-g)) * u * column[:, w : w + 1]
            hid[rows, w * UNITS : (w + 1) * UNITS] = value.astype(BF16)

    def cols_of(j, cy):
        return pl.ds(pl.multiple_of(cy * QUARTER + (j % 2) * WIDE, 128), WIDE)

    def down_product(j, cy):
        cols = cols_of(j, cy)
        right = jnp.concatenate([ws[6 + w, cols, :] for w in range(EXPERTS)], axis=1)
        total = lax.dot_general(
            hid[...], right, (((1,), (1,)), ((), ())), preferred_element_type=F32
        )
        part[:, :, :, cols] = total.astype(BF16).reshape(N, N, ROWS, WIDE)
        for i, d in enumerate((1, 3, 2)):
            if j % 2 == 0:
                src = part.at[ring(x, d), :, :, cols]
            else:
                src = part.at[:, ring(z, d), :, cols]
            send(src, r1.at[i, :, :, cols], rrecv1.at[j, i], along(j % 2, d))

    def sum_first(j, cy):
        cols = cols_of(j, cy)
        own = part[x, :, :, cols] if j % 2 == 0 else part[:, z, :, cols]
        total = own.astype(F32)
        for i in range(3):
            arrived(r1.at[i, :, :, cols], rrecv1.at[j, i])
            total = total + r1[i, :, :, cols].astype(F32)
        s1[:, :, cols] = total.astype(BF16)
        for i, d in enumerate((1, 3, 2)):
            to = ring(z, d) if j % 2 == 0 else ring(x, d)
            send(s1.at[to, :, cols], r2.at[i, :, cols], rrecv2.at[j, i], along(1 - j % 2, d))

    def sum_second(j, cy):
        cols = cols_of(j, cy)
        total = s1[z if j % 2 == 0 else x, :, cols].astype(F32)
        for i in range(3):
            arrived(r2.at[i, :, cols], rrecv2.at[j, i])
            total = total + r2[i, :, cols].astype(F32)
        out[:, cols] = total.astype(BF16)

    order = [y, y, before, before, after, after, across, across]
    for j in range(PIECES):
        if j % 2 == 0:
            if j == 6:
                hand_over_far(1)
            from_partner(1, order[j])
        down_product(j, order[j])
    for j in range(PIECES):
        sum_first(j, order[j])
    for j in range(PIECES):
        sum_second(j, order[j])

    for cp in sends:
        cp.wait_send()
    arrived(ws.at[0:6, 0 : 15 * DEPTH, :], asend.at[0])
    arrived(ws.at[6:9, 0 : 15 * DEPTH, :], asend.at[1])


SENDS = 1 + 30 + 28 + 48


def local(tokens, expert_ids, gate_scores, gate_weight, up_weight, down_weight):
    any_space = pl.BlockSpec(memory_space=pl.ANY)
    vmem = pl.BlockSpec(memory_space=pltpu.VMEM)
    dma = pltpu.SemaphoreType.DMA
    return pl.pallas_call(
        kernel,
        out_shape=jax.ShapeDtypeStruct((ROWS, D), BF16),
        in_specs=[any_space, vmem, vmem, any_space, any_space, any_space],
        out_specs=vmem,
        scratch_shapes=[
            pltpu.VMEM((N, N, ROWS, D), BF16),
            pltpu.VMEM((3 * EXPERTS, D, UNITS), BF16),
            pltpu.VMEM((EXPERTS, N * N * ROWS, 2 * UNITS), F32),
            pltpu.VMEM((N * N * ROWS, EXPERTS * UNITS), BF16),
            pltpu.VMEM((N, N, ROWS, D), BF16),
            pltpu.VMEM((3, N, ROWS, D), BF16),
            pltpu.VMEM((N, ROWS, D), BF16),
            pltpu.VMEM((3, ROWS, D), BF16),
            pltpu.VMEM((2, 8, 256), F32),
            dma((SENDS,)),
            dma((2,)),
            dma((2, 2)),
            dma((2, 16)),
            dma((2, N, N)),
            dma,
            dma((PIECES, 3)),
            dma((PIECES, 3)),
            dma,
        ],
        compiler_params=pltpu.CompilerParams(
            collective_id=0, has_side_effects=True, vmem_limit_bytes=64000 * 1024
        ),
        name="relay_experts",
    )(tokens, expert_ids.T, gate_scores.T, gate_weight, up_weight, down_weight)


def solution(mesh):
    return jax.shard_map(
        local,
        mesh=mesh,
        in_specs=(
            P(("expert", "tensor"), None),
            P("expert", None),
            P("expert", None),
            P(None, ("expert", "tensor"), None),
            P(None, ("expert", "tensor"), None),
            P(None, ("expert", "tensor"), None),
        ),
        out_specs=P(("expert", "tensor"), None),
        check_vma=False,
    )
```

```python
import jax
import jax.numpy as jnp
from jax import lax
from jax.experimental import pallas as pl
from jax.experimental.pallas import tpu as pltpu
from jax.sharding import PartitionSpec as P

MESH = pl.DeviceIdType.MESH
F32 = jnp.float32
BF16 = jnp.bfloat16

N = 4
EXPERTS = 3
D = 7168
ROWS = 32
DEPTH = 56
CHUNK = 448
QUARTER = 1792
UNITS = 128
HALF = D // 2
PIECES = 8
WIDE = D // PIECES
LAG = 2

PLANE = (
    (1, 0), (3, 0), (0, 1), (0, 3), (2, 0), (0, 2), (1, 1), (3, 3),
    (2, 1), (1, 3), (3, 1), (2, 3), (1, 2), (3, 2), (2, 2),
)


def place():
    e = lax.axis_index("expert")
    t = lax.axis_index("tensor")
    y, xl, c = lax.div(e, 4), lax.rem(lax.div(e, 2), 2), lax.rem(e, 2)
    xh, z = lax.div(t, 4), lax.rem(t, 4)
    return e, t, y, xh * 2 + xl, z, c, xl, xh


def device(y, x, z, c):
    return {
        "expert": y * 4 + lax.rem(x, 2) * 2 + c,
        "tensor": lax.div(x, 2) * 4 + z,
    }


def ring(v, d):
    return lax.rem(v + d, N)


def kernel(
    tok, ids, scores, gate, up, down, out,
    xs, ws, acc, hid, part, ra, r1, s1, rb, r2, comb,
    ssem, asend, arecv, wrecv, trecv, crecv, rrecv1, rrecv2, lsem,
):
    e, t, y, x, z, c, xl, xh = place()
    mine = e * 8 + t
    sends = []

    def send(src, dst, recv, to):
        cp = pltpu.make_async_remote_copy(
            src_ref=src,
            dst_ref=dst,
            send_sem=ssem.at[len(sends)],
            recv_sem=recv,
            device_id=to,
            device_id_type=MESH,
        )
        cp.start()
        sends.append(cp)

    def arrived(ref, sem):
        pltpu.make_async_copy(ref, ref, sem).wait()

    which = lax.broadcasted_iota(jnp.int32, (8, 256), 0)
    marks = scores[...].astype(F32)
    first, second = marks[0:1, :], marks[1:2, :]
    picked = jnp.where(ids[0:1, :] == which, first, 0.0) + jnp.where(
        ids[1:2, :] == which, second, 0.0
    )
    comb[xl] = picked / (first + second)

    barrier = pltpu.get_barrier_semaphore()
    peers = [device(y, ring(x, dx), ring(z, dz), c) for dx, dz in PLANE]
    north, south = device(ring(y, 1), x, z, c), device(ring(y, 3), x, z, c)
    partner = device(y, x, z, 1 - c)
    for to in [*peers, north, south, partner]:
        pl.semaphore_signal(barrier, inc=1, device_id=to, device_id_type=MESH)
    pl.semaphore_wait(barrier, len(peers) + 3)

    own_rows = pl.ds(pl.multiple_of(mine * DEPTH, 8), DEPTH)

    def columns(px, pz):
        return pl.ds(pl.multiple_of((px * N + pz) * UNITS, UNITS), UNITS)

    def spread(ref, lo, kind):
        for (dx, dz), to in zip(PLANE, peers):
            cols = columns(ring(x, dx), ring(z, dz))
            pltpu.make_async_remote_copy(
                src_ref=ref.at[:, :, cols],
                dst_ref=ws.at[lo : lo + EXPERTS, own_rows, :],
                send_sem=asend.at[kind],
                recv_sem=arecv.at[kind, xl],
                device_id=to,
                device_id_type=MESH,
            ).start()

    def keep(ref, lo, kind):
        pltpu.make_async_copy(
            ref.at[:, :, columns(x, z)],
            ws.at[lo : lo + EXPERTS, own_rows, :],
            arecv.at[kind, xl],
        ).start()

    own_tok = pltpu.make_async_copy(tok, xs.at[x, z], lsem)
    own_tok.start()
    keep(gate, 0, 0)
    keep(up, 3, 0)
    keep(down, 6, 1)
    spread(gate, 0, 0)
    spread(up, 3, 0)
    other = device(y, xh * 2 + 1 - xl, z, c)
    send(comb.at[xl], comb.at[xl], crecv, other)

    def along(axis, d):
        if axis == 0:
            return device(y, ring(x, d), z, c)
        return device(y, x, ring(z, d), c)

    halves = (pl.ds(0, HALF), pl.ds(HALF, HALF))
    ALL, LOW, HIGH = pl.ds(0, ROWS), pl.ds(0, ROWS // 2), pl.ds(ROWS // 2, ROWS // 2)

    def block(half, a, b):
        if half == 0:
            return ring(x, a), ring(z, b)
        return ring(x, b), ring(z, a)

    def send_tokens(half, leg, a, b, d, rows=ALL, src=None):
        bx, bz = block(half, a, b)
        cols = halves[half]
        dst = xs.at[bx, bz, rows, cols]
        to = along(leg if half == 0 else 1 - leg, d)
        send(dst if src is None else src.at[rows, cols], dst, trecv.at[half, bx, bz], to)

    def wait_tokens(half, a, b):
        bx, bz = block(half, a, b)
        arrived(xs.at[bx, bz, :, halves[half]], trecv.at[half, bx, bz])

    for leg in range(2):
        for half in range(2):
            for d in (1, 3):
                send_tokens(half, leg, 0, 0, d, src=tok)
    spread(down, 6, 1)

    bounds = ((0, 6), (6, 9))

    def chunk(kind, cy, cx, cc):
        lo, hi = bounds[kind]
        k = cy * 4 + cx * 2 + cc
        rows = pl.ds(pl.multiple_of(k * CHUNK, CHUNK), CHUNK)
        return ws.at[lo:hi, rows, :], wrecv.at[kind, k]

    def pass_on(kind, cy, cx, to):
        ref, sem = chunk(kind, cy, cx, c)
        send(ref, ref, sem, to)

    def wait_chunk(kind, cy, cx, cc):
        ref, sem = chunk(kind, cy, cx, cc)
        arrived(ref, sem)

    def own_chunks(kind):
        arrived(chunk(kind, y, 0, c)[0], arecv.at[kind, 0])
        pass_on(kind, y, 0, north)
        pass_on(kind, y, 0, partner)
        arrived(chunk(kind, y, 1, c)[0], arecv.at[kind, 1])
        pass_on(kind, y, 1, south)
        pass_on(kind, y, 1, north)
        pass_on(kind, y, 0, south)
        pass_on(kind, y, 1, partner)

    before, after, across = ring(y, 3), ring(y, 1), ring(y, 2)

    def relay(kind):
        wait_chunk(kind, before, 0, c)
        pass_on(kind, before, 0, north)
        pass_on(kind, before, 0, partner)
        wait_chunk(kind, after, 1, c)
        pass_on(kind, after, 1, south)
        pass_on(kind, after, 1, partner)

    def hand_over(kind):
        wait_chunk(kind, before, 1, c)
        pass_on(kind, before, 1, partner)
        wait_chunk(kind, after, 0, c)
        pass_on(kind, after, 0, partner)

    def hand_over_far(kind):
        for cx in range(2):
            wait_chunk(kind, across, cx, c)
            pass_on(kind, across, cx, partner)

    def from_partner(kind, cy):
        for cx in range(2):
            wait_chunk(kind, cy, cx, 1 - c)

    def second_leg(half, a):
        send_tokens(half, 1, a, 0, 1)
        send_tokens(half, 1, a, 0, 3)

    def second_relay(half, a):
        wait_tokens(half, a, 3)
        if a in (0, 3):
            send_tokens(half, 1, a, 3, 1)
        wait_tokens(half, a, 1)
        if a in (1, 2):
            send_tokens(half, 1, a, 1, 3)

    own_chunks(0)
    for half in range(2):
        wait_tokens(half, 3, 0)
        send_tokens(half, 0, 3, 0, 1, LOW)
        second_leg(half, 3)
    for half in range(2):
        wait_tokens(half, 1, 0)
        send_tokens(half, 0, 1, 0, 3, HIGH)
        second_leg(half, 1)
    for half in range(2):
        second_relay(half, 0)
    for half in range(2):
        wait_tokens(half, 2, 0)
        second_leg(half, 2)
    relay(0)
    own_chunks(1)
    for a in (3, 1, 2):
        for half in range(2):
            second_relay(half, a)
    hand_over(0)
    own_tok.wait()
    for a in range(N):
        for half in range(2):
            wait_tokens(half, a, 2)

    def products(cy, start):
        span = pl.ds(pl.multiple_of(cy * QUARTER, 256), QUARTER)

        def one(w, carry):
            left = xs[:, :, :, span].reshape(N * N * ROWS, QUARTER)
            right = jnp.concatenate([ws[w, span, :], ws[EXPERTS + w, span, :]], axis=1)
            total = jnp.dot(left, right, preferred_element_type=F32)
            acc[w] = total if start else acc[w] + total
            return carry

        lax.fori_loop(0, EXPERTS, one, 0)

    from_partner(0, y)
    products(y, True)
    from_partner(0, before)
    products(before, False)
    from_partner(0, after)
    products(after, False)
    relay(1)
    hand_over_far(0)
    hand_over(1)
    from_partner(0, across)
    products(across, False)

    arrived(comb.at[1 - xl], crecv)
    for bx in range(N):
        column = comb[bx % 2][:, (bx // 2) * 128 : (bx // 2) * 128 + 128].T
        rows = slice(bx * N * ROWS, (bx + 1) * N * ROWS)
        for w in range(EXPERTS):
            g = acc[w, rows, 0:UNITS]
            u = acc[w, rows, UNITS : 2 * UNITS]
            value = g / (1.0 + jnp.exp(-g)) * u * column[:, w : w + 1]
            hid[rows, w * UNITS : (w + 1) * UNITS] = value.astype(BF16)

    def cols_of(j, cy):
        return pl.ds(pl.multiple_of(cy * QUARTER + (j % 2) * WIDE, 128), WIDE)

    def down_product(j, cy):
        cols = cols_of(j, cy)
        right = jnp.concatenate([ws[6 + w, cols, :] for w in range(EXPERTS)], axis=1)
        total = lax.dot_general(
            hid[...], right, (((1,), (1,)), ((), ())), preferred_element_type=F32
        )
        part[:, :, :, cols] = total.astype(BF16).reshape(N, N, ROWS, WIDE)

    def add_into(ref, more):
        ref[...] = (ref[...].astype(F32) + more[...].astype(F32)).astype(BF16)

    def share(axis, b, half, cols):
        if axis == 0:
            return part.at[b, 2 * half : 2 * half + 2, :, cols]
        return part.at[2 * half : 2 * half + 2, b, :, cols]

    def first_send(j, cy):
        down_product(j, cy)
        cols, axis = cols_of(j, cy), j % 2
        me = (x, z)[axis]
        sem = lambda i: rrecv1.at[j, i]
        far = ring(me, 2)
        send(share(axis, far, 0, cols), ra.at[0, :, :, cols], sem(0), along(axis, 1))
        send(share(axis, far, 1, cols), ra.at[1, :, :, cols], sem(1), along(axis, 3))
        send(share(axis, ring(me, 1), 1, cols), r1.at[0, 2:4, :, cols], sem(2), along(axis, 1))
        send(share(axis, ring(me, 3), 0, cols), r1.at[1, 0:2, :, cols], sem(3), along(axis, 3))

    def first_relay(j, cy):
        cols, axis = cols_of(j, cy), j % 2
        me = (x, z)[axis]
        for i, d in enumerate((1, 3)):
            more = ra.at[i, :, :, cols]
            arrived(more, rrecv1.at[j, i])
            ref = share(axis, ring(me, d), i, cols)
            add_into(ref, more)
            send(ref, r1.at[i, 2 * i : 2 * i + 2, :, cols], rrecv1.at[j, 4 + i], along(axis, d))

    def first_sum(j, cy):
        cols, axis = cols_of(j, cy), j % 2
        own = part[x, :, :, cols] if axis == 0 else part[:, z, :, cols]
        total = own.astype(F32)
        for i in range(2):
            arrived(r1.at[i, 2 - 2 * i : 4 - 2 * i, :, cols], rrecv1.at[j, 2 + i])
            arrived(r1.at[i, 2 * i : 2 * i + 2, :, cols], rrecv1.at[j, 4 + i])
            total = total + r1[i, :, :, cols].astype(F32)
        s1[:, :, cols] = total.astype(BF16)
        me, axis = (z, x)[axis], 1 - axis
        far = ring(me, 2)
        sem = lambda i: rrecv2.at[j, i]
        send(s1.at[far, LOW, cols], rb.at[0, :, cols], sem(0), along(axis, 1))
        send(s1.at[far, HIGH, cols], rb.at[1, :, cols], sem(1), along(axis, 3))
        send(s1.at[ring(me, 1), HIGH, cols], r2.at[0, HIGH, cols], sem(2), along(axis, 1))
        send(s1.at[ring(me, 3), LOW, cols], r2.at[1, LOW, cols], sem(3), along(axis, 3))

    def second_relay_sum(j, cy):
        cols, axis = cols_of(j, cy), 1 - j % 2
        me = (x, z)[axis]
        for i, d in enumerate((1, 3)):
            rows = (LOW, HIGH)[i]
            more = rb.at[i, :, cols]
            arrived(more, rrecv2.at[j, i])
            ref = s1.at[ring(me, d), rows, cols]
            add_into(ref, more)
            send(ref, r2.at[i, rows, cols], rrecv2.at[j, 4 + i], along(axis, d))

    def second_sum(j, cy):
        cols, axis = cols_of(j, cy), 1 - j % 2
        total = s1[(x, z)[axis], :, cols].astype(F32)
        for i in range(2):
            arrived(r2.at[i, (HIGH, LOW)[i], cols], rrecv2.at[j, 2 + i])
            arrived(r2.at[i, (LOW, HIGH)[i], cols], rrecv2.at[j, 4 + i])
            total = total + r2[i, :, cols].astype(F32)
        out[:, cols] = total.astype(BF16)

    order = [y, y, before, before, after, after, across, across]
    stages = (first_send, first_relay, first_sum, second_relay_sum, second_sum)
    for n in range(PIECES + LAG * (len(stages) - 1)):
        if n < PIECES and n % 2 == 0:
            if n == 6:
                hand_over_far(1)
            from_partner(1, order[n])
        for i, stage in enumerate(stages):
            j = n - LAG * i
            if 0 <= j < PIECES:
                stage(j, order[j])

    for cp in sends:
        cp.wait_send()
    arrived(ws.at[0:6, 0 : 15 * DEPTH, :], asend.at[0])
    arrived(ws.at[6:9, 0 : 15 * DEPTH, :], asend.at[1])


SENDS = 1 + 16 + 4 + 12 + 4 + 28 + 96 + 8


def local(tokens, expert_ids, gate_scores, gate_weight, up_weight, down_weight):
    any_space = pl.BlockSpec(memory_space=pl.ANY)
    vmem = pl.BlockSpec(memory_space=pltpu.VMEM)
    dma = pltpu.SemaphoreType.DMA
    return pl.pallas_call(
        kernel,
        out_shape=jax.ShapeDtypeStruct((ROWS, D), BF16),
        in_specs=[any_space, vmem, vmem, any_space, any_space, any_space],
        out_specs=vmem,
        scratch_shapes=[
            pltpu.VMEM((N, N, ROWS, D), BF16),
            pltpu.VMEM((3 * EXPERTS, D, UNITS), BF16),
            pltpu.VMEM((EXPERTS, N * N * ROWS, 2 * UNITS), F32),
            pltpu.VMEM((N * N * ROWS, EXPERTS * UNITS), BF16),
            pltpu.VMEM((N, N, ROWS, D), BF16),
            pltpu.VMEM((2, N // 2, ROWS, D), BF16),
            pltpu.VMEM((2, N, ROWS, D), BF16),
            pltpu.VMEM((N, ROWS, D), BF16),
            pltpu.VMEM((2, ROWS // 2, D), BF16),
            pltpu.VMEM((2, ROWS, D), BF16),
            pltpu.VMEM((2, 8, 256), F32),
            dma((SENDS,)),
            dma((2,)),
            dma((2, 2)),
            dma((2, 16)),
            dma((2, N, N)),
            dma,
            dma((PIECES, 6)),
            dma((PIECES, 6)),
            dma,
        ],
        compiler_params=pltpu.CompilerParams(
            collective_id=0, has_side_effects=True, vmem_limit_bytes=64000 * 1024
        ),
        name="relay_experts",
    )(tokens, expert_ids.T, gate_scores.T, gate_weight, up_weight, down_weight)


def solution(mesh):
    return jax.shard_map(
        local,
        mesh=mesh,
        in_specs=(
            P(("expert", "tensor"), None),
            P("expert", None),
            P("expert", None),
            P(None, ("expert", "tensor"), None),
            P(None, ("expert", "tensor"), None),
            P(None, ("expert", "tensor"), None),
        ),
        out_specs=P(("expert", "tensor"), None),
        check_vma=False,
    )
```

```python
import jax
import jax.numpy as jnp
from jax import lax
from jax.experimental import pallas as pl
from jax.experimental.pallas import tpu as pltpu
from jax.sharding import PartitionSpec as P

MESH = pl.DeviceIdType.MESH
F32 = jnp.float32
BF16 = jnp.bfloat16

N = 4
EXPERTS = 3
D = 7168
FF = 2048
ROWS = 32
GROUP = N * N * ROWS
DEPTH = 56
CHUNK = 448
QUARTER = 1792
UNITS = 128
SPAN = 896

PLANE = (
    (1, 0), (3, 0), (0, 1), (0, 3), (2, 0), (0, 2), (1, 1), (3, 3),
    (2, 1), (1, 3), (3, 1), (2, 3), (1, 2), (3, 2), (2, 2),
)


def place():
    e = lax.axis_index("expert")
    t = lax.axis_index("tensor")
    y, xl, c = lax.div(e, 4), lax.rem(lax.div(e, 2), 2), lax.rem(e, 2)
    xh, z = lax.div(t, 4), lax.rem(t, 4)
    return e, t, y, xh * 2 + xl, z, c, xl, xh


def device(y, x, z, c):
    return {
        "expert": y * 4 + lax.rem(x, 2) * 2 + c,
        "tensor": lax.div(x, 2) * 4 + z,
    }


def ring(v, d):
    return lax.rem(v + d, N)


def kernel(
    tok, ids, scores, gate, up, down, out,
    xs, wg, wd, acc, hb, mask, total_ref, ob, back, order_ref, info,
    ssem, asend, arecv, wrecv, drecv, trecv, hrecv, irecv, osem, lsem,
):
    e_index, t_index, y, x, z, c, xl, xh = place()
    mine = e_index * 8 + t_index
    sends = []

    def send(src, dst, recv, to):
        cp = pltpu.make_async_remote_copy(
            src_ref=src,
            dst_ref=dst,
            send_sem=ssem.at[len(sends)],
            recv_sem=recv,
            device_id=to,
            device_id_type=MESH,
        )
        cp.start()
        sends.append(cp)

    def arrived(ref, sem):
        pltpu.make_async_copy(ref, ref, sem).wait()

    barrier = pltpu.get_barrier_semaphore()
    peers = [device(y, ring(x, dx), ring(z, dz), c) for dx, dz in PLANE]
    north, south = device(ring(y, 1), x, z, c), device(ring(y, 3), x, z, c)
    partner = device(y, x, z, 1 - c)
    for to in [*peers, north, south, partner]:
        pl.semaphore_signal(barrier, inc=1, device_id=to, device_id_type=MESH)

    marks = scores[...].astype(F32)
    info[xl, 0:2, :] = ids[...].astype(F32)
    info[xl, 2:4, :] = marks / (marks[0:1, :] + marks[1:2, :])

    own_rows = pl.ds(pl.multiple_of(mine * DEPTH, 8), DEPTH)
    before, after, across = ring(y, 3), ring(y, 1), ring(y, 2)

    def columns(px, pz):
        return pl.ds(pl.multiple_of((px * N + pz) * UNITS, UNITS), UNITS)

    own_tok = pltpu.make_async_copy(tok, xs.at[x, z], lsem)
    own_tok.start()
    for w in range(EXPERTS):
        for i, ref in enumerate((gate, up)):
            pltpu.make_async_copy(
                ref.at[w, :, columns(x, z)], wg.at[2 * w + i, own_rows, :], arecv.at[w, xl]
            ).start()

    def down_piece(w, cy, cc, cols=slice(None)):
        rows = pl.ds(pl.multiple_of(cc * DEPTH, 8), DEPTH)
        return wd.at[w, cy, rows, cols]

    own_down = []
    for w in range(EXPERTS):
        cp = pltpu.make_async_copy(down.at[w], down_piece(w, y, c), drecv.at[w, y, c])
        cp.start()
        own_down.append(cp)

    pl.semaphore_wait(barrier, len(peers) + 3)

    def down_own(w):
        for to in (north, south, partner):
            send(down.at[w], down_piece(w, y, c), drecv.at[w, y, c], to)

    def down_pass(w, cy, to, cols=slice(None)):
        ref = down_piece(w, cy, c, cols)
        send(ref, ref, drecv.at[w, cy, c], to)

    def down_wait(w, cy, cc):
        arrived(down_piece(w, cy, cc), drecv.at[w, cy, cc])

    def down_relay(w):
        down_wait(w, before, c)
        down_pass(w, before, north, slice(0, FF // 2))
        down_wait(w, after, c)
        down_pass(w, after, south, slice(FF // 2, FF))
        down_pass(w, before, partner)
        down_pass(w, after, partner)

    def down_far(w):
        down_wait(w, across, c)
        down_pass(w, across, partner)

    def spread(w):
        for (dx, dz), to in zip(PLANE, peers):
            cols = columns(ring(x, dx), ring(z, dz))
            for i, ref in enumerate((gate, up)):
                pltpu.make_async_remote_copy(
                    src_ref=ref.at[w, :, cols],
                    dst_ref=wg.at[2 * w + i, own_rows, :],
                    send_sem=asend.at[w],
                    recv_sem=arecv.at[w, xl],
                    device_id=to,
                    device_id_type=MESH,
                ).start()

    def chunk(w, cy, cx, cc):
        k = cy * 4 + cx * 2 + cc
        rows = pl.ds(pl.multiple_of(k * CHUNK, CHUNK), CHUNK)
        return wg.at[2 * w : 2 * w + 2, rows, :], wrecv.at[w, k]

    def pass_on(w, cy, cx, to):
        ref, sem = chunk(w, cy, cx, c)
        send(ref, ref, sem, to)

    def wait_chunk(w, cy, cx, cc):
        ref, sem = chunk(w, cy, cx, cc)
        arrived(ref, sem)

    def own_chunks(w):
        arrived(chunk(w, y, 0, c)[0], arecv.at[w, 0])
        pass_on(w, y, 0, north)
        arrived(chunk(w, y, 1, c)[0], arecv.at[w, 1])
        pass_on(w, y, 1, south)
        pass_on(w, y, 1, north)
        pass_on(w, y, 0, south)
        pass_on(w, y, 0, partner)
        pass_on(w, y, 1, partner)

    def relay(w):
        wait_chunk(w, before, 0, c)
        pass_on(w, before, 0, north)
        wait_chunk(w, after, 1, c)
        pass_on(w, after, 1, south)
        pass_on(w, before, 0, partner)
        pass_on(w, after, 1, partner)

    def hand_over(w):
        wait_chunk(w, before, 1, c)
        pass_on(w, before, 1, partner)
        wait_chunk(w, after, 0, c)
        pass_on(w, after, 0, partner)

    def hand_over_far(w):
        for cx in range(2):
            wait_chunk(w, across, cx, c)
            pass_on(w, across, cx, partner)

    def from_partner(w):
        for cy in (y, before, after, across):
            for cx in range(2):
                wait_chunk(w, cy, cx, 1 - c)

    class Gather:
        def __init__(self, ref, sem, whole, low, high):
            self.ref, self.sem, self.whole, self.low, self.high = ref, sem, whole, low, high

        def block(self, half, a, b):
            return (ring(x, a), ring(z, b)) if half == 0 else (ring(x, b), ring(z, a))

        def to(self, half, leg, d):
            if (half + leg) % 2 == 0:
                return device(y, ring(x, d), z, c)
            return device(y, x, ring(z, d), c)

        def send(self, half, leg, a, b, d, part=None, src=None):
            bx, bz = self.block(half, a, b)
            part = (part or self.whole)[half]
            dst = self.ref.at[bx, bz, part[0], part[1]]
            src = dst if src is None else src.at[part[0], part[1]]
            send(src, dst, self.sem.at[half, bx, bz], self.to(half, leg, d))

        def wait(self, half, a, b):
            bx, bz = self.block(half, a, b)
            part = self.whole[half]
            arrived(self.ref.at[bx, bz, part[0], part[1]], self.sem.at[half, bx, bz])

        def start(self, src=None):
            for leg in range(2):
                for half in range(2):
                    for d in (1, 3):
                        self.send(half, leg, 0, 0, d, src=src)

        def near(self, a):
            for half in range(2):
                self.wait(half, a, 0)
                if a == 3:
                    self.send(half, 0, 3, 0, 1, self.low)
                elif a == 1:
                    self.send(half, 0, 1, 0, 3, self.high)
                self.send(half, 1, a, 0, 1)
                self.send(half, 1, a, 0, 3)

        def relay(self, a):
            for half in range(2):
                self.wait(half, a, 3)
                if a in (0, 3):
                    self.send(half, 1, a, 3, 1)
                self.wait(half, a, 1)
                if a in (1, 2):
                    self.send(half, 1, a, 1, 3)

        def far(self, a):
            for half in range(2):
                self.wait(half, a, 2)

    rows_all = pl.ds(0, ROWS)
    sides = (pl.ds(0, D // 2), pl.ds(D // 2, D // 2))
    upper, lower = pl.ds(0, ROWS // 2), pl.ds(ROWS // 2, ROWS // 2)
    tokens = Gather(
        xs, trecv,
        [(rows_all, s) for s in sides],
        [(upper, s) for s in sides],
        [(lower, s) for s in sides],
    )
    every = pl.ds(0, 2 * UNITS)
    fourths = [pl.ds(i * GROUP // 4, GROUP // 4) for i in range(4)]
    hidden = Gather(
        hb, hrecv,
        [(pl.ds(i * GROUP // 2, GROUP // 2), every) for i in range(2)],
        [(fourths[0], every), (fourths[2], every)],
        [(fourths[1], every), (fourths[3], every)],
    )

    down_own(0)
    spread(0)
    spread(1)
    send(info.at[xl], info.at[xl], irecv, device(y, xh * 2 + 1 - xl, z, c))
    tokens.start(tok)
    spread(2)

    wd[:, :, 2 * DEPTH :, :] = jnp.zeros((EXPERTS, N, 128 - 2 * DEPTH, FF), BF16)
    lane = lax.broadcasted_iota(jnp.int32, (128, SPAN), 0)
    wanted = lax.broadcasted_iota(jnp.int32, (128, SPAN), 1)
    for q in range(8):
        spot = jnp.where(lane < DEPTH, lane, lane + CHUNK - DEPTH) + q * DEPTH
        spot = jnp.where(lane < 2 * DEPTH, spot, -1)
        order_ref[q * 128 : (q + 1) * 128, :] = jnp.where(spot == wanted, 1.0, 0.0).astype(BF16)

    arrived(info.at[1 - xl], irecv)
    route = []
    for bx in range(N):
        column = info[bx % 2][:, (bx // 2) * 128 : (bx // 2) * 128 + 128].T
        route.append(column)
        rows = slice(bx * N * ROWS, (bx + 1) * N * ROWS)
        for k in range(2):
            for w in range(EXPERTS):
                hit = jnp.where(column[:, k : k + 1] == float(w), 1.0, 0.0)
                mask[k, w, rows, :] = jnp.broadcast_to(hit, (N * ROWS, UNITS)).astype(BF16)

    own_chunks(0)
    own_chunks(1)
    relay(0)
    tokens.near(3)
    tokens.near(1)
    tokens.relay(0)
    hand_over(0)
    own_chunks(2)
    tokens.near(2)
    relay(1)
    hand_over_far(0)
    down_own(1)
    down_own(2)
    tokens.relay(3)
    tokens.relay(1)
    hand_over(1)
    relay(2)
    tokens.relay(2)
    down_relay(0)
    own_tok.wait()
    for a in range(N):
        tokens.far(a)

    def products(w):
        def one(q, carry):
            span = pl.ds(pl.multiple_of(q * QUARTER, 256), QUARTER)
            left = xs[:, :, :, span].reshape(GROUP, QUARTER)
            right = jnp.concatenate([wg[2 * w, span, :], wg[2 * w + 1, span, :]], axis=1)
            acc[w] += jnp.dot(left, right, preferred_element_type=F32)
            return carry

        acc[w] = jnp.zeros((GROUP, 2 * UNITS), F32)
        lax.fori_loop(0, N, one, 0)

    from_partner(0)
    products(0)
    hand_over_far(1)
    from_partner(1)
    products(1)
    hand_over(2)
    hand_over_far(2)
    from_partner(2)
    products(2)

    for bx in range(N):
        rows = slice(bx * N * ROWS, (bx + 1) * N * ROWS)
        values = []
        for w in range(EXPERTS):
            g = acc[w, rows, 0:UNITS]
            u = acc[w, rows, UNITS : 2 * UNITS]
            values.append(g / (1.0 + jnp.exp(-g)) * u)
        column = info[bx % 2][:, (bx // 2) * 128 : (bx // 2) * 128 + 128].T
        for k in range(2):
            chosen = column[:, k : k + 1]
            value = jnp.where(chosen == 0.0, values[0], jnp.where(chosen == 1.0, values[1], values[2]))
            value = value * column[:, 2 + k : 3 + k]
            hb[x, z, rows, k * UNITS : (k + 1) * UNITS] = value.astype(BF16)

    def down_products(half, a):
        rows = pl.ds(half * GROUP // 2, GROUP // 2)
        left, right = [], []
        for b in range(N):
            bx, bz = hidden.block(half, a, b)
            one, two = hb[bx, bz, rows, 0:UNITS], hb[bx, bz, rows, UNITS : 2 * UNITS]
            for w in range(EXPERTS):
                left.append(one * mask[0, w, rows, :] + two * mask[1, w, rows, :])
                right.append(wd[w, :, :, columns(bx, bz)].reshape(N * 128, UNITS))
        more = lax.dot_general(
            jnp.concatenate(left, axis=1), jnp.concatenate(right, axis=1),
            (((1,), (1,)), ((), ())), preferred_element_type=F32,
        )
        total_ref[rows, :] = more if a == 0 else total_ref[rows, :] + more

    hidden.start()
    down_relay(1)
    hidden.near(3)
    hidden.near(1)
    hidden.relay(0)
    down_relay(2)
    hidden.near(2)
    for w in range(EXPERTS):
        down_far(w)
    hidden.relay(3)
    hidden.relay(1)
    hidden.relay(2)
    for w in range(EXPERTS):
        own_down[w].wait()
        for cy in (y, before, after, across):
            down_wait(w, cy, 1 - c)
    for a in (0, 3, 1, 2):
        hidden.far(a)
        for half in range(2):
            down_products(half, a)

    for cy in range(N):
        piece = total_ref[:, cy * 128 : (cy + 1) * 128].astype(BF16)
        ob[:, :, cy, :, :] = piece.reshape(N, N, ROWS, 128)
    spot = back.at[xl, :, :, pl.ds(pl.multiple_of(t_index * 128, 128), 128)]
    for (dx, dz), to in zip(PLANE, peers):
        send(ob.at[ring(x, dx), ring(z, dz)], spot, osem, to)
    pltpu.make_async_copy(ob.at[x, z], spot, osem).start()
    arrived(back, osem)
    result = jnp.dot(
        back[...].reshape(2 * N * ROWS, 8 * 128), order_ref[...], preferred_element_type=F32
    ).astype(BF16)
    for cx in range(2):
        for cy in range(N):
            k = cx * N + cy
            base = (cy * 2 + cx) * SPAN
            out[:, base : base + SPAN] = result[k * ROWS : (k + 1) * ROWS, :]

    for cp in sends:
        cp.wait_send()
    for w in range(EXPERTS):
        arrived(wg.at[0:2, 0 : 15 * DEPTH, :], asend.at[w])


SENDS = 146


def local(tokens, expert_ids, gate_scores, gate_weight, up_weight, down_weight):
    any_space = pl.BlockSpec(memory_space=pl.ANY)
    vmem = pl.BlockSpec(memory_space=pltpu.VMEM)
    dma = pltpu.SemaphoreType.DMA
    return pl.pallas_call(
        kernel,
        out_shape=jax.ShapeDtypeStruct((ROWS, D), BF16),
        in_specs=[any_space, vmem, vmem, any_space, any_space, any_space],
        out_specs=vmem,
        scratch_shapes=[
            pltpu.VMEM((N, N, ROWS, D), BF16),
            pltpu.VMEM((2 * EXPERTS, D, UNITS), BF16),
            pltpu.VMEM((EXPERTS, N, 128, FF), BF16),
            pltpu.VMEM((EXPERTS, GROUP, 2 * UNITS), F32),
            pltpu.VMEM((N, N, GROUP, 2 * UNITS), BF16),
            pltpu.VMEM((2, EXPERTS, GROUP, UNITS), BF16),
            pltpu.VMEM((GROUP, N * 128), F32),
            pltpu.VMEM((N, N, N, ROWS, 128), BF16),
            pltpu.VMEM((2, N, ROWS, 8 * 128), BF16),
            pltpu.VMEM((8 * 128, SPAN), BF16),
            pltpu.VMEM((2, 8, 256), F32),
            dma((SENDS,)),
            dma((EXPERTS,)),
            dma((EXPERTS, 2)),
            dma((EXPERTS, 16)),
            dma((EXPERTS, N, 2)),
            dma((2, N, N)),
            dma((2, N, N)),
            dma,
            dma,
            dma,
        ],
        compiler_params=pltpu.CompilerParams(
            collective_id=0, has_side_effects=True, vmem_limit_bytes=64000 * 1024
        ),
        name="relay_experts",
    )(tokens, expert_ids.T, gate_scores.T, gate_weight, up_weight, down_weight)


def solution(mesh):
    return jax.shard_map(
        local,
        mesh=mesh,
        in_specs=(
            P(("expert", "tensor"), None),
            P("expert", None),
            P("expert", None),
            P(None, ("expert", "tensor"), None),
            P(None, ("expert", "tensor"), None),
            P(None, ("expert", "tensor"), None),
        ),
        out_specs=P(("expert", "tensor"), None),
        check_vma=False,
    )
```

```python
import jax
import jax.numpy as jnp
from jax import lax
from jax.experimental import pallas as pl
from jax.experimental.pallas import tpu as pltpu
from jax.sharding import PartitionSpec as P

MESH = pl.DeviceIdType.MESH
F32 = jnp.float32
BF16 = jnp.bfloat16

N = 4
EXPERTS = 3
D = 7168
FF = 2048
ROWS = 32
GROUP = N * N * ROWS
DEPTH = 56
CHUNK = 448
QUARTER = 1792
UNITS = 128
SPAN = 896

PLANE = (
    (1, 0), (3, 0), (0, 1), (0, 3), (2, 0), (0, 2), (1, 1), (3, 3),
    (2, 1), (1, 3), (3, 1), (2, 3), (1, 2), (3, 2), (2, 2),
)


def place():
    e = lax.axis_index("expert")
    t = lax.axis_index("tensor")
    y, xl, c = lax.div(e, 4), lax.rem(lax.div(e, 2), 2), lax.rem(e, 2)
    xh, z = lax.div(t, 4), lax.rem(t, 4)
    return e, t, y, xh * 2 + xl, z, c, xl, xh


def device(y, x, z, c):
    return {
        "expert": y * 4 + lax.rem(x, 2) * 2 + c,
        "tensor": lax.div(x, 2) * 4 + z,
    }


def ring(v, d):
    return lax.rem(v + d, N)


def kernel(
    tok, ids, scores, gate, up, down, out,
    xs, wg, wd, acc, hb, mask, total_ref, ob, back, order_ref, info,
    ssem, asend, arecv, wrecv, drecv, trecv, hrecv, irecv, osem, fsem, lsem,
):
    e_index, t_index, y, x, z, c, xl, xh = place()
    mine = e_index * 8 + t_index
    sends = []

    def send(src, dst, recv, to):
        cp = pltpu.make_async_remote_copy(
            src_ref=src,
            dst_ref=dst,
            send_sem=ssem.at[len(sends)],
            recv_sem=recv,
            device_id=to,
            device_id_type=MESH,
        )
        cp.start()
        sends.append(cp)

    def arrived(ref, sem):
        pltpu.make_async_copy(ref, ref, sem).wait()

    barrier = pltpu.get_barrier_semaphore()
    peers = [device(y, ring(x, dx), ring(z, dz), c) for dx, dz in PLANE]
    north, south = device(ring(y, 1), x, z, c), device(ring(y, 3), x, z, c)
    partner = device(y, x, z, 1 - c)
    for to in [*peers, north, south, partner]:
        pl.semaphore_signal(barrier, inc=1, device_id=to, device_id_type=MESH)

    marks = scores[...].astype(F32)
    info[xl, 0:2, :] = ids[...].astype(F32)
    info[xl, 2:4, :] = marks / (marks[0:1, :] + marks[1:2, :])

    own_rows = pl.ds(pl.multiple_of(mine * DEPTH, 8), DEPTH)
    before, after, across = ring(y, 3), ring(y, 1), ring(y, 2)

    def columns(px, pz):
        return pl.ds(pl.multiple_of((px * N + pz) * UNITS, UNITS), UNITS)

    own_tok = pltpu.make_async_copy(tok, xs.at[x, z], lsem)
    own_tok.start()
    for w in range(EXPERTS):
        for i, ref in enumerate((gate, up)):
            pltpu.make_async_copy(
                ref.at[w, :, columns(x, z)], wg.at[2 * w + i, own_rows, :], arecv.at[w, xl]
            ).start()

    def down_piece(w, cy, cc, cols=slice(None)):
        rows = pl.ds(pl.multiple_of(cc * DEPTH, 8), DEPTH)
        return wd.at[w, cy, rows, cols]

    own_down = []
    for w in range(EXPERTS):
        cp = pltpu.make_async_copy(down.at[w], down_piece(w, y, c), drecv.at[w, y, c])
        cp.start()
        own_down.append(cp)

    pl.semaphore_wait(barrier, len(peers) + 3)

    def down_own(w):
        for to in (north, south, partner):
            send(down.at[w], down_piece(w, y, c), drecv.at[w, y, c], to)

    def down_pass(w, cy, to, cols=slice(None)):
        ref = down_piece(w, cy, c, cols)
        send(ref, ref, drecv.at[w, cy, c], to)

    def down_wait(w, cy, cc):
        arrived(down_piece(w, cy, cc), drecv.at[w, cy, cc])

    def down_relay(w):
        down_wait(w, before, c)
        down_pass(w, before, north, slice(0, FF // 2))
        down_wait(w, after, c)
        down_pass(w, after, south, slice(FF // 2, FF))
        down_pass(w, before, partner)
        down_pass(w, after, partner)

    def down_far(w):
        down_wait(w, across, c)
        down_pass(w, across, partner)

    def spread(w):
        for (dx, dz), to in zip(PLANE, peers):
            cols = columns(ring(x, dx), ring(z, dz))
            for i, ref in enumerate((gate, up)):
                pltpu.make_async_remote_copy(
                    src_ref=ref.at[w, :, cols],
                    dst_ref=wg.at[2 * w + i, own_rows, :],
                    send_sem=asend.at[w],
                    recv_sem=arecv.at[w, xl],
                    device_id=to,
                    device_id_type=MESH,
                ).start()

    def chunk(w, cy, cx, cc):
        k = cy * 4 + cx * 2 + cc
        rows = pl.ds(pl.multiple_of(k * CHUNK, CHUNK), CHUNK)
        return wg.at[pl.ds(2 * w, 2), rows, :], wrecv.at[w, k]

    def pass_on(w, cy, cx, to):
        ref, sem = chunk(w, cy, cx, c)
        send(ref, ref, sem, to)

    def wait_chunk(w, cy, cx, cc):
        ref, sem = chunk(w, cy, cx, cc)
        arrived(ref, sem)

    def own_chunks(w):
        arrived(chunk(w, y, 0, c)[0], arecv.at[w, 0])
        pass_on(w, y, 0, north)
        arrived(chunk(w, y, 1, c)[0], arecv.at[w, 1])
        pass_on(w, y, 1, south)
        pass_on(w, y, 1, north)
        pass_on(w, y, 0, south)
        pass_on(w, y, 0, partner)
        pass_on(w, y, 1, partner)

    def relay(w):
        wait_chunk(w, before, 0, c)
        pass_on(w, before, 0, north)
        wait_chunk(w, after, 1, c)
        pass_on(w, after, 1, south)
        pass_on(w, before, 0, partner)
        pass_on(w, after, 1, partner)

    def hand_over(w):
        wait_chunk(w, before, 1, c)
        pass_on(w, before, 1, partner)
        wait_chunk(w, after, 0, c)
        pass_on(w, after, 0, partner)

    def hand_over_far(w):
        for cx in range(2):
            wait_chunk(w, across, cx, c)
            pass_on(w, across, cx, partner)

    def from_partner(w, cy):
        for cx in range(2):
            wait_chunk(w, cy, cx, 1 - c)

    class Gather:
        def __init__(self, ref, sem, whole, low, high):
            self.ref, self.sem, self.whole, self.low, self.high = ref, sem, whole, low, high

        def block(self, half, a, b):
            return (ring(x, a), ring(z, b)) if half == 0 else (ring(x, b), ring(z, a))

        def to(self, half, leg, d):
            if (half + leg) % 2 == 0:
                return device(y, ring(x, d), z, c)
            return device(y, x, ring(z, d), c)

        def send(self, half, leg, a, b, d, part=None, src=None):
            bx, bz = self.block(half, a, b)
            part = (part or self.whole)[half]
            dst = self.ref.at[bx, bz, part[0], part[1]]
            src = dst if src is None else src.at[part[0], part[1]]
            send(src, dst, self.sem.at[half, bx, bz], self.to(half, leg, d))

        def wait(self, half, a, b):
            bx, bz = self.block(half, a, b)
            part = self.whole[half]
            arrived(self.ref.at[bx, bz, part[0], part[1]], self.sem.at[half, bx, bz])

        def start(self, src=None):
            for leg in range(2):
                for half in range(2):
                    for d in (1, 3):
                        self.send(half, leg, 0, 0, d, src=src)

        def near(self, a):
            for half in range(2):
                self.wait(half, a, 0)
                if a == 3:
                    self.send(half, 0, 3, 0, 1, self.low)
                elif a == 1:
                    self.send(half, 0, 1, 0, 3, self.high)
                self.send(half, 1, a, 0, 1)
                self.send(half, 1, a, 0, 3)

        def relay(self, a):
            for half in range(2):
                self.wait(half, a, 3)
                if a in (0, 3):
                    self.send(half, 1, a, 3, 1)
                self.wait(half, a, 1)
                if a in (1, 2):
                    self.send(half, 1, a, 1, 3)

        def far(self, a):
            for half in range(2):
                self.wait(half, a, 2)

    rows_all = pl.ds(0, ROWS)
    upper, lower = pl.ds(0, ROWS // 2), pl.ds(ROWS // 2, ROWS // 2)

    def token_gather(i):
        sides = [pl.ds((2 * i + j) * QUARTER, QUARTER) for j in range(2)]
        return Gather(
            xs, trecv.at[i],
            [(rows_all, s) for s in sides],
            [(upper, s) for s in sides],
            [(lower, s) for s in sides],
        )

    every = pl.ds(0, 2 * UNITS)

    def hidden_gather(i):
        part = lambda lo, n: pl.ds(i * GROUP // 2 + lo, n)
        return Gather(
            hb, hrecv.at[i],
            [(part(0, 128), every), (part(128, 128), every)],
            [(part(0, 64), every), (part(128, 64), every)],
            [(part(64, 64), every), (part(192, 64), every)],
        )

    tok_a, tok_b = token_gather(0), token_gather(1)
    hid_a, hid_b = hidden_gather(0), hidden_gather(1)

    down_own(0)
    spread(0)
    send(info.at[xl], info.at[xl], irecv, device(y, xh * 2 + 1 - xl, z, c))
    tok_a.start(tok)

    wd[:, :, 2 * DEPTH :, :] = jnp.zeros((EXPERTS, N, 128 - 2 * DEPTH, FF), BF16)
    lane = lax.broadcasted_iota(jnp.int32, (128, SPAN), 0)
    wanted = lax.broadcasted_iota(jnp.int32, (128, SPAN), 1)
    for q in range(8):
        spot = jnp.where(lane < DEPTH, lane, lane + CHUNK - DEPTH) + q * DEPTH
        spot = jnp.where(lane < 2 * DEPTH, spot, -1)
        order_ref[q * 128 : (q + 1) * 128, :] = jnp.where(spot == wanted, 1.0, 0.0).astype(BF16)

    arrived(info.at[1 - xl], irecv)
    route = []
    for bx in range(N):
        column = info[bx % 2][:, (bx // 2) * 128 : (bx // 2) * 128 + 128].T
        route.append(column)
        rows = slice(bx * N * ROWS, (bx + 1) * N * ROWS)
        for k in range(2):
            for w in range(EXPERTS):
                hit = jnp.where(column[:, k : k + 1] == float(w), 1.0, 0.0)
                mask[k, w, rows, :] = jnp.broadcast_to(hit, (N * ROWS, UNITS)).astype(BF16)

    def quarter(w, q):
        span = pl.ds(pl.multiple_of(q * QUARTER, 256), QUARTER)
        left = xs[:, :, :, span].reshape(GROUP, QUARTER)
        right = jnp.concatenate([wg[2 * w, span, :], wg[2 * w + 1, span, :]], axis=1)
        acc[w] += jnp.dot(left, right, preferred_element_type=F32)

    def products(w, first):
        def one(q, carry):
            quarter(w, q)
            return carry

        lax.fori_loop(first, first + 2, one, 0)

    def all_from_partner(w):
        for cy in (y, before, after, across):
            from_partner(w, cy)

    def tokens_a_here():
        for a in range(N):
            tok_a.far(a)
        own_tok.wait()

    def tokens_b_here():
        for a in range(N):
            tok_b.far(a)

    acc[...] = jnp.zeros((EXPERTS, GROUP, 2 * UNITS), F32)
    own_chunks(0)
    spread(1)
    tok_a.near(3)
    tok_a.near(1)
    spread(2)
    tok_b.start(tok)
    relay(0)
    own_chunks(1)
    tok_a.relay(0)
    tok_a.near(2)
    tok_a.relay(3)
    tok_a.relay(1)
    hand_over(0)
    relay(1)
    tok_b.near(3)
    tok_b.near(1)
    own_chunks(2)
    tok_a.relay(2)
    hand_over_far(0)
    tok_b.relay(0)
    tok_b.near(2)
    hand_over(1)
    tokens_a_here()
    all_from_partner(0)
    products(0, 0)
    tok_b.relay(3)
    tok_b.relay(1)
    relay(2)
    down_own(1)
    down_own(2)
    hand_over_far(1)
    tok_b.relay(2)
    all_from_partner(1)
    products(1, 0)
    tokens_b_here()
    products(0, 2)
    products(1, 2)

    hand_over(2)
    hand_over_far(2)
    for cy in (y, before, after, across):
        from_partner(2, cy)
    products(2, 0)
    products(2, 2)

    for bx in range(N):
        rows = slice(bx * N * ROWS, (bx + 1) * N * ROWS)
        values = []
        for w in range(EXPERTS):
            g = acc[w, rows, 0:UNITS]
            u = acc[w, rows, UNITS : 2 * UNITS]
            values.append(g / (1.0 + jnp.exp(-g)) * u)
        column = info[bx % 2][:, (bx // 2) * 128 : (bx // 2) * 128 + 128].T
        for k in range(2):
            chosen = column[:, k : k + 1]
            value = jnp.where(chosen == 0.0, values[0], jnp.where(chosen == 1.0, values[1], values[2]))
            value = value * column[:, 2 + k : 3 + k]
            hb[x, z, rows, k * UNITS : (k + 1) * UNITS] = value.astype(BF16)

    near_blocks = [(a, b) for a in (0, 3, 1) for b in (0, 3, 1)]
    far_blocks = [(2, 0), (0, 2), (2, 3), (3, 2), (2, 1), (1, 2), (2, 2)]

    def down_products(i, blocks, start):
        rows = pl.ds(i * GROUP // 2, GROUP // 2)
        left, right = [], []
        for a, b in blocks:
            bx, bz = ring(x, a), ring(z, b)
            one, two = hb[bx, bz, rows, 0:UNITS], hb[bx, bz, rows, UNITS : 2 * UNITS]
            for w in range(EXPERTS):
                left.append(one * mask[0, w, rows, :] + two * mask[1, w, rows, :])
                right.append(wd[w, :, :, columns(bx, bz)].reshape(N * 128, UNITS))
        more = lax.dot_general(
            jnp.concatenate(left, axis=1), jnp.concatenate(right, axis=1),
            (((1,), (1,)), ((), ())), preferred_element_type=F32,
        )
        if start:
            total_ref[rows, :] = more
            return
        more = more + total_ref[rows, :]
        for cy in range(N):
            piece = more[:, cy * 128 : (cy + 1) * 128].astype(BF16)
            ob[2 * i : 2 * i + 2, :, cy, :, :] = piece.reshape(2, N, ROWS, 128)

    spot = back.at[xl, :, :, pl.ds(pl.multiple_of(t_index * 128, 128), 128)]

    def give_back(i):
        for near in (1, 0):
            bx = 2 * i + lax.rem(x + near, 2)
            for d in (1, 3, 2, 0):
                if near == 0 and d == 0:
                    continue
                bz = ring(z, d)
                send(ob.at[bx, bz], spot, osem, device(y, bx, bz, c))

        @pl.when(i == xh)
        def _():
            pltpu.make_async_copy(ob.at[x, z], spot, osem).start()

        @pl.when(i != xh)
        def _():
            pltpu.make_async_remote_copy(
                src_ref=ob.at[ring(x, 2), z],
                dst_ref=spot,
                send_sem=fsem,
                recv_sem=osem,
                device_id=device(y, ring(x, 2), z, c),
                device_id_type=MESH,
            ).start()

    hid_a.start()
    hid_b.start()
    hid_a.near(3)
    hid_a.near(1)
    down_relay(0)
    hid_a.relay(0)
    hid_a.near(2)
    hid_b.near(3)
    hid_b.near(1)
    down_relay(1)
    hid_a.relay(3)
    hid_a.relay(1)
    hid_b.relay(0)
    down_relay(2)
    hid_b.near(2)
    hid_a.relay(2)
    hid_b.relay(3)
    hid_b.relay(1)
    for w in range(EXPERTS):
        down_far(w)
    hid_b.relay(2)
    for w in range(EXPERTS):
        own_down[w].wait()
        for cy in (y, before, after, across):
            down_wait(w, cy, 1 - c)
    down_products(0, near_blocks, True)
    for a in range(N):
        hid_a.far(a)
    down_products(0, far_blocks, False)
    give_back(0)
    down_products(1, near_blocks, True)
    for a in range(N):
        hid_b.far(a)
    down_products(1, far_blocks, False)
    give_back(1)
    arrived(back, osem)
    result = jnp.dot(
        back[...].reshape(2 * N * ROWS, 8 * 128), order_ref[...], preferred_element_type=F32
    ).astype(BF16)
    for cx in range(2):
        for cy in range(N):
            k = cx * N + cy
            base = (cy * 2 + cx) * SPAN
            out[:, base : base + SPAN] = result[k * ROWS : (k + 1) * ROWS, :]

    for cp in sends:
        cp.wait_send()
    arrived(ob.at[ring(x, 2), z], fsem)
    for w in range(EXPERTS):
        arrived(wg.at[0:2, 0 : 15 * DEPTH, :], asend.at[w])


SENDS = 212


def local(tokens, expert_ids, gate_scores, gate_weight, up_weight, down_weight):
    any_space = pl.BlockSpec(memory_space=pl.ANY)
    vmem = pl.BlockSpec(memory_space=pltpu.VMEM)
    dma = pltpu.SemaphoreType.DMA
    return pl.pallas_call(
        kernel,
        out_shape=jax.ShapeDtypeStruct((ROWS, D), BF16),
        in_specs=[any_space, vmem, vmem, any_space, any_space, any_space],
        out_specs=vmem,
        scratch_shapes=[
            pltpu.VMEM((N, N, ROWS, D), BF16),
            pltpu.VMEM((2 * EXPERTS, D, UNITS), BF16),
            pltpu.VMEM((EXPERTS, N, 128, FF), BF16),
            pltpu.VMEM((EXPERTS, GROUP, 2 * UNITS), F32),
            pltpu.VMEM((N, N, GROUP, 2 * UNITS), BF16),
            pltpu.VMEM((2, EXPERTS, GROUP, UNITS), BF16),
            pltpu.VMEM((GROUP, N * 128), F32),
            pltpu.VMEM((N, N, N, ROWS, 128), BF16),
            pltpu.VMEM((2, N, ROWS, 8 * 128), BF16),
            pltpu.VMEM((8 * 128, SPAN), BF16),
            pltpu.VMEM((2, 8, 256), F32),
            dma((SENDS,)),
            dma((EXPERTS,)),
            dma((EXPERTS, 2)),
            dma((EXPERTS, 16)),
            dma((EXPERTS, N, 2)),
            dma((2, 2, N, N)),
            dma((2, 2, N, N)),
            dma,
            dma,
            dma,
            dma,
        ],
        compiler_params=pltpu.CompilerParams(
            collective_id=0, has_side_effects=True, vmem_limit_bytes=64000 * 1024
        ),
        name="relay_experts",
    )(tokens, expert_ids.T, gate_scores.T, gate_weight, up_weight, down_weight)


def solution(mesh):
    return jax.shard_map(
        local,
        mesh=mesh,
        in_specs=(
            P(("expert", "tensor"), None),
            P("expert", None),
            P("expert", None),
            P(None, ("expert", "tensor"), None),
            P(None, ("expert", "tensor"), None),
            P(None, ("expert", "tensor"), None),
        ),
        out_specs=P(("expert", "tensor"), None),
        check_vma=False,
    )
```

```python
import jax
import jax.numpy as jnp
from jax import lax
from jax.experimental import pallas as pl
from jax.experimental.pallas import tpu as pltpu
from jax.sharding import PartitionSpec as P

MESH = pl.DeviceIdType.MESH
F32 = jnp.float32
BF16 = jnp.bfloat16

N = 4
EXPERTS = 3
D = 7168
FF = 2048
ROWS = 32
GROUP = N * N * ROWS
DEPTH = 56
CHUNK = 448
QUARTER = 1792
UNITS = 128
SPAN = 896

PLANE = (
    (1, 0), (3, 0), (0, 1), (0, 3), (2, 0), (0, 2), (1, 1), (3, 3),
    (2, 1), (1, 3), (3, 1), (2, 3), (1, 2), (3, 2), (2, 2),
)


def place():
    e = lax.axis_index("expert")
    t = lax.axis_index("tensor")
    y, xl, c = lax.div(e, 4), lax.rem(lax.div(e, 2), 2), lax.rem(e, 2)
    xh, z = lax.div(t, 4), lax.rem(t, 4)
    return e, t, y, xh * 2 + xl, z, c, xl, xh


def device(y, x, z, c):
    return {
        "expert": y * 4 + lax.rem(x, 2) * 2 + c,
        "tensor": lax.div(x, 2) * 4 + z,
    }


def ring(v, d):
    return lax.rem(v + d, N)


def kernel(
    tok, ids, scores, gate, up, down, out,
    xs, wg, wd, acc, hb, mask, total_ref, ob, back, order_ref, info,
    ssem, asend, arecv, wrecv, drecv, trecv, hrecv, irecv, osem, fsem, lsem,
):
    e_index, t_index, y, x, z, c, xl, xh = place()
    mine = e_index * 8 + t_index
    sends = []

    def send(src, dst, recv, to):
        cp = pltpu.make_async_remote_copy(
            src_ref=src,
            dst_ref=dst,
            send_sem=ssem.at[len(sends)],
            recv_sem=recv,
            device_id=to,
            device_id_type=MESH,
        )
        cp.start()
        sends.append(cp)

    def arrived(ref, sem):
        pltpu.make_async_copy(ref, ref, sem).wait()

    barrier = pltpu.get_barrier_semaphore()
    peers = [device(y, ring(x, dx), ring(z, dz), c) for dx, dz in PLANE]
    north, south = device(ring(y, 1), x, z, c), device(ring(y, 3), x, z, c)
    partner = device(y, x, z, 1 - c)
    for to in [*peers, north, south, partner]:
        pl.semaphore_signal(barrier, inc=1, device_id=to, device_id_type=MESH)

    marks = scores[...].astype(F32)
    info[xl, 0:2, :] = ids[...].astype(F32)
    info[xl, 2:4, :] = marks / (marks[0:1, :] + marks[1:2, :])

    own_rows = pl.ds(pl.multiple_of(mine * DEPTH, 8), DEPTH)
    before, after, across = ring(y, 3), ring(y, 1), ring(y, 2)

    def columns(px, pz):
        return pl.ds(pl.multiple_of((px * N + pz) * UNITS, UNITS), UNITS)

    own_tok = pltpu.make_async_copy(tok, xs.at[x, z], lsem)
    own_tok.start()
    for w in range(EXPERTS):
        for i, ref in enumerate((gate, up)):
            pltpu.make_async_copy(
                ref.at[w, :, columns(x, z)], wg.at[i, w, own_rows, :], arecv.at[min(w, 1), xl]
            ).start()

    def down_piece(w, cy, cc, cols=slice(None)):
        rows = pl.ds(pl.multiple_of(cc * DEPTH, 8), DEPTH)
        return wd.at[w, cy, rows, cols]

    own_down = []
    for w in range(EXPERTS):
        cp = pltpu.make_async_copy(down.at[w], down_piece(w, y, c), drecv.at[w, y, c])
        cp.start()
        own_down.append(cp)

    pl.semaphore_wait(barrier, len(peers) + 3)

    def down_own(w):
        for to in (north, south, partner):
            send(down.at[w], down_piece(w, y, c), drecv.at[w, y, c], to)

    def down_pass(w, cy, to, cols=slice(None)):
        ref = down_piece(w, cy, c, cols)
        send(ref, ref, drecv.at[w, cy, c], to)

    def down_wait(w, cy, cc):
        arrived(down_piece(w, cy, cc), drecv.at[w, cy, cc])

    def down_relay(w):
        down_wait(w, before, c)
        down_pass(w, before, north, slice(0, FF // 2))
        down_wait(w, after, c)
        down_pass(w, after, south, slice(FF // 2, FF))
        down_pass(w, before, partner)
        down_pass(w, after, partner)

    def down_far(w):
        down_wait(w, across, c)
        down_pass(w, across, partner)

    sets = (pl.ds(0, 1), pl.ds(1, EXPERTS - 1))

    def spread(k):
        for (dx, dz), to in zip(PLANE, peers):
            cols = columns(ring(x, dx), ring(z, dz))
            for i, ref in enumerate((gate, up)):
                pltpu.make_async_remote_copy(
                    src_ref=ref.at[sets[k], :, cols],
                    dst_ref=wg.at[i, sets[k], own_rows, :],
                    send_sem=asend.at[k],
                    recv_sem=arecv.at[k, xl],
                    device_id=to,
                    device_id_type=MESH,
                ).start()

    def chunk(w, cy, cx, cc):
        k = cy * 4 + cx * 2 + cc
        rows = pl.ds(pl.multiple_of(k * CHUNK, CHUNK), CHUNK)
        return wg.at[:, w, rows, :], wrecv.at[w, k]

    def pass_on(w, cy, cx, to):
        ref, sem = chunk(w, cy, cx, c)
        send(ref, ref, sem, to)

    def wait_chunk(w, cy, cx, cc):
        ref, sem = chunk(w, cy, cx, cc)
        arrived(ref, sem)

    def spread_here(k, cx):
        rows = pl.ds(pl.multiple_of((y * 4 + cx * 2 + c) * CHUNK, CHUNK), CHUNK)
        arrived(wg.at[:, sets[k], rows, :], arecv.at[k, cx])

    def own_chunks(w):
        if w < 2:
            spread_here(w, 0)
        pass_on(w, y, 0, north)
        if w < 2:
            spread_here(w, 1)
        pass_on(w, y, 1, south)
        pass_on(w, y, 1, north)
        pass_on(w, y, 0, south)
        pass_on(w, y, 0, partner)
        pass_on(w, y, 1, partner)

    def relay(w):
        wait_chunk(w, before, 0, c)
        pass_on(w, before, 0, north)
        wait_chunk(w, after, 1, c)
        pass_on(w, after, 1, south)
        pass_on(w, before, 0, partner)
        pass_on(w, after, 1, partner)

    def hand_over(w):
        wait_chunk(w, before, 1, c)
        pass_on(w, before, 1, partner)
        wait_chunk(w, after, 0, c)
        pass_on(w, after, 0, partner)

    def hand_over_far(w):
        for cx in range(2):
            wait_chunk(w, across, cx, c)
            pass_on(w, across, cx, partner)

    def from_partner(w, cy):
        for cx in range(2):
            wait_chunk(w, cy, cx, 1 - c)

    class Gather:
        def __init__(self, ref, sem, whole, low, high):
            self.ref, self.sem, self.whole, self.low, self.high = ref, sem, whole, low, high

        def block(self, half, a, b):
            return (ring(x, a), ring(z, b)) if half == 0 else (ring(x, b), ring(z, a))

        def to(self, half, leg, d):
            if (half + leg) % 2 == 0:
                return device(y, ring(x, d), z, c)
            return device(y, x, ring(z, d), c)

        def send(self, half, leg, a, b, d, part=None, src=None):
            bx, bz = self.block(half, a, b)
            part = (part or self.whole)[half]
            dst = self.ref.at[bx, bz, part[0], part[1]]
            src = dst if src is None else src.at[part[0], part[1]]
            send(src, dst, self.sem.at[half, bx, bz], self.to(half, leg, d))

        def wait(self, half, a, b):
            bx, bz = self.block(half, a, b)
            part = self.whole[half]
            arrived(self.ref.at[bx, bz, part[0], part[1]], self.sem.at[half, bx, bz])

        def start(self, src=None):
            for leg in range(2):
                for half in range(2):
                    for d in (1, 3):
                        self.send(half, leg, 0, 0, d, src=src)

        def near(self, a):
            for half in range(2):
                self.wait(half, a, 0)
                if a == 3:
                    self.send(half, 0, 3, 0, 1, self.low)
                elif a == 1:
                    self.send(half, 0, 1, 0, 3, self.high)
                self.send(half, 1, a, 0, 1)
                self.send(half, 1, a, 0, 3)

        def relay(self, a):
            for half in range(2):
                self.wait(half, a, 3)
                if a in (0, 3):
                    self.send(half, 1, a, 3, 1)
                self.wait(half, a, 1)
                if a in (1, 2):
                    self.send(half, 1, a, 1, 3)

        def far(self, a):
            for half in range(2):
                self.wait(half, a, 2)

    rows_all = pl.ds(0, ROWS)
    upper, lower = pl.ds(0, ROWS // 2), pl.ds(ROWS // 2, ROWS // 2)

    def token_gather(i):
        sides = [pl.ds((2 * i + j) * QUARTER, QUARTER) for j in range(2)]
        return Gather(
            xs, trecv.at[i],
            [(rows_all, s) for s in sides],
            [(upper, s) for s in sides],
            [(lower, s) for s in sides],
        )

    every = pl.ds(0, 2 * UNITS)

    def hidden_gather(i):
        part = lambda lo, n: pl.ds(i * GROUP // 2 + lo, n)
        return Gather(
            hb, hrecv.at[i],
            [(part(0, 128), every), (part(128, 128), every)],
            [(part(0, 64), every), (part(128, 64), every)],
            [(part(64, 64), every), (part(192, 64), every)],
        )

    tok_a, tok_b = token_gather(0), token_gather(1)
    hid_a, hid_b = hidden_gather(0), hidden_gather(1)

    down_own(0)
    spread(0)
    send(info.at[xl], info.at[xl], irecv, device(y, xh * 2 + 1 - xl, z, c))
    tok_a.start(tok)

    wd[:, :, 2 * DEPTH :, :] = jnp.zeros((EXPERTS, N, 128 - 2 * DEPTH, FF), BF16)
    lane = lax.broadcasted_iota(jnp.int32, (128, SPAN), 0)
    wanted = lax.broadcasted_iota(jnp.int32, (128, SPAN), 1)
    for q in range(8):
        spot = jnp.where(lane < DEPTH, lane, lane + CHUNK - DEPTH) + q * DEPTH
        spot = jnp.where(lane < 2 * DEPTH, spot, -1)
        order_ref[q * 128 : (q + 1) * 128, :] = jnp.where(spot == wanted, 1.0, 0.0).astype(BF16)

    arrived(info.at[1 - xl], irecv)
    route = []
    for bx in range(N):
        column = info[bx % 2][:, (bx // 2) * 128 : (bx // 2) * 128 + 128].T
        route.append(column)
        rows = slice(bx * N * ROWS, (bx + 1) * N * ROWS)
        for k in range(2):
            for w in range(EXPERTS):
                hit = jnp.where(column[:, k : k + 1] == float(w), 1.0, 0.0)
                mask[k, w, rows, :] = jnp.broadcast_to(hit, (N * ROWS, UNITS)).astype(BF16)

    def quarter(w, q):
        span = pl.ds(pl.multiple_of(q * QUARTER, 256), QUARTER)
        left = xs[:, :, :, span].reshape(GROUP, QUARTER)
        right = jnp.concatenate([wg[0, w, span, :], wg[1, w, span, :]], axis=1)
        acc[w] += jnp.dot(left, right, preferred_element_type=F32)

    def products(w, first):
        def one(q, carry):
            quarter(w, q)
            return carry

        lax.fori_loop(first, first + 2, one, 0)

    def all_from_partner(w):
        for cy in (y, before, after, across):
            from_partner(w, cy)

    def tokens_a_here():
        for a in range(N):
            tok_a.far(a)
        own_tok.wait()

    def tokens_b_here():
        for a in range(N):
            tok_b.far(a)

    acc[...] = jnp.zeros((EXPERTS, GROUP, 2 * UNITS), F32)
    own_chunks(0)
    spread(1)
    tok_a.near(3)
    tok_a.near(1)
    tok_b.start(tok)
    relay(0)
    own_chunks(1)
    tok_a.relay(0)
    tok_a.near(2)
    tok_a.relay(3)
    tok_a.relay(1)
    hand_over(0)
    relay(1)
    tok_b.near(3)
    tok_b.near(1)
    own_chunks(2)
    tok_a.relay(2)
    hand_over_far(0)
    tok_b.relay(0)
    tok_b.near(2)
    hand_over(1)
    tokens_a_here()
    all_from_partner(0)
    products(0, 0)
    tok_b.relay(3)
    tok_b.relay(1)
    relay(2)
    down_own(1)
    down_own(2)
    hand_over_far(1)
    tok_b.relay(2)
    all_from_partner(1)
    products(1, 0)
    tokens_b_here()
    products(0, 2)
    products(1, 2)

    hand_over(2)
    hand_over_far(2)
    for cy in (y, before, after, across):
        from_partner(2, cy)
    products(2, 0)
    products(2, 2)

    for bx in range(N):
        rows = slice(bx * N * ROWS, (bx + 1) * N * ROWS)
        values = []
        for w in range(EXPERTS):
            g = acc[w, rows, 0:UNITS]
            u = acc[w, rows, UNITS : 2 * UNITS]
            values.append(g / (1.0 + jnp.exp(-g)) * u)
        column = info[bx % 2][:, (bx // 2) * 128 : (bx // 2) * 128 + 128].T
        for k in range(2):
            chosen = column[:, k : k + 1]
            value = jnp.where(chosen == 0.0, values[0], jnp.where(chosen == 1.0, values[1], values[2]))
            value = value * column[:, 2 + k : 3 + k]
            hb[x, z, rows, k * UNITS : (k + 1) * UNITS] = value.astype(BF16)

    near_blocks = [(a, b) for a in (0, 3, 1) for b in (0, 3, 1)]
    far_blocks = [(2, 0), (0, 2), (2, 3), (3, 2), (2, 1), (1, 2), (2, 2)]

    def down_products(i, blocks, start):
        rows = pl.ds(i * GROUP // 2, GROUP // 2)
        left, right = [], []
        for a, b in blocks:
            bx, bz = ring(x, a), ring(z, b)
            one, two = hb[bx, bz, rows, 0:UNITS], hb[bx, bz, rows, UNITS : 2 * UNITS]
            for w in range(EXPERTS):
                left.append(one * mask[0, w, rows, :] + two * mask[1, w, rows, :])
                right.append(wd[w, :, :, columns(bx, bz)].reshape(N * 128, UNITS))
        more = lax.dot_general(
            jnp.concatenate(left, axis=1), jnp.concatenate(right, axis=1),
            (((1,), (1,)), ((), ())), preferred_element_type=F32,
        )
        if start:
            total_ref[rows, :] = more
            return
        more = more + total_ref[rows, :]
        for cy in range(N):
            piece = more[:, cy * 128 : (cy + 1) * 128].astype(BF16)
            ob[2 * i : 2 * i + 2, :, cy, :, :] = piece.reshape(2, N, ROWS, 128)

    spot = back.at[xl, :, :, pl.ds(pl.multiple_of(t_index * 128, 128), 128)]

    def give_back(i):
        for near in (1, 0):
            bx = 2 * i + lax.rem(x + near, 2)
            for d in (1, 3, 2, 0):
                if near == 0 and d == 0:
                    continue
                bz = ring(z, d)
                send(ob.at[bx, bz], spot, osem, device(y, bx, bz, c))

        @pl.when(i == xh)
        def _():
            pltpu.make_async_copy(ob.at[x, z], spot, osem).start()

        @pl.when(i != xh)
        def _():
            pltpu.make_async_remote_copy(
                src_ref=ob.at[ring(x, 2), z],
                dst_ref=spot,
                send_sem=fsem,
                recv_sem=osem,
                device_id=device(y, ring(x, 2), z, c),
                device_id_type=MESH,
            ).start()

    hid_a.start()
    hid_b.start()
    hid_a.near(3)
    hid_a.near(1)
    down_relay(0)
    hid_a.relay(0)
    hid_a.near(2)
    hid_b.near(3)
    hid_b.near(1)
    down_relay(1)
    hid_a.relay(3)
    hid_a.relay(1)
    hid_b.relay(0)
    down_relay(2)
    hid_b.near(2)
    hid_a.relay(2)
    hid_b.relay(3)
    hid_b.relay(1)
    for w in range(EXPERTS):
        down_far(w)
    hid_b.relay(2)
    for w in range(EXPERTS):
        own_down[w].wait()
        for cy in (y, before, after, across):
            down_wait(w, cy, 1 - c)
    down_products(0, near_blocks, True)
    for a in range(N):
        hid_a.far(a)
    down_products(0, far_blocks, False)
    give_back(0)
    down_products(1, near_blocks, True)
    for a in range(N):
        hid_b.far(a)
    down_products(1, far_blocks, False)
    give_back(1)
    arrived(back, osem)
    result = jnp.dot(
        back[...].reshape(2 * N * ROWS, 8 * 128), order_ref[...], preferred_element_type=F32
    ).astype(BF16)
    for cx in range(2):
        for cy in range(N):
            k = cx * N + cy
            base = (cy * 2 + cx) * SPAN
            out[:, base : base + SPAN] = result[k * ROWS : (k + 1) * ROWS, :]

    for cp in sends:
        cp.wait_send()
    arrived(ob.at[ring(x, 2), z], fsem)
    for k in range(2):
        arrived(wg.at[:, sets[k], 0 : 15 * DEPTH, :], asend.at[k])


SENDS = 212


def local(tokens, expert_ids, gate_scores, gate_weight, up_weight, down_weight):
    any_space = pl.BlockSpec(memory_space=pl.ANY)
    vmem = pl.BlockSpec(memory_space=pltpu.VMEM)
    dma = pltpu.SemaphoreType.DMA
    return pl.pallas_call(
        kernel,
        out_shape=jax.ShapeDtypeStruct((ROWS, D), BF16),
        in_specs=[any_space, vmem, vmem, any_space, any_space, any_space],
        out_specs=vmem,
        scratch_shapes=[
            pltpu.VMEM((N, N, ROWS, D), BF16),
            pltpu.VMEM((2, EXPERTS, D, UNITS), BF16),
            pltpu.VMEM((EXPERTS, N, 128, FF), BF16),
            pltpu.VMEM((EXPERTS, GROUP, 2 * UNITS), F32),
            pltpu.VMEM((N, N, GROUP, 2 * UNITS), BF16),
            pltpu.VMEM((2, EXPERTS, GROUP, UNITS), BF16),
            pltpu.VMEM((GROUP, N * 128), F32),
            pltpu.VMEM((N, N, N, ROWS, 128), BF16),
            pltpu.VMEM((2, N, ROWS, 8 * 128), BF16),
            pltpu.VMEM((8 * 128, SPAN), BF16),
            pltpu.VMEM((2, 8, 256), F32),
            dma((SENDS,)),
            dma((2,)),
            dma((2, 2)),
            dma((EXPERTS, 16)),
            dma((EXPERTS, N, 2)),
            dma((2, 2, N, N)),
            dma((2, 2, N, N)),
            dma,
            dma,
            dma,
            dma,
        ],
        compiler_params=pltpu.CompilerParams(
            collective_id=0, has_side_effects=True, vmem_limit_bytes=64000 * 1024
        ),
        name="relay_experts",
    )(tokens, expert_ids.T, gate_scores.T, gate_weight, up_weight, down_weight)


def solution(mesh):
    return jax.shard_map(
        local,
        mesh=mesh,
        in_specs=(
            P(("expert", "tensor"), None),
            P("expert", None),
            P("expert", None),
            P(None, ("expert", "tensor"), None),
            P(None, ("expert", "tensor"), None),
            P(None, ("expert", "tensor"), None),
        ),
        out_specs=P(("expert", "tensor"), None),
        check_vma=False,
    )
```

```python
import jax
import jax.numpy as jnp
from jax import lax
from jax.experimental import pallas as pl
from jax.experimental.pallas import tpu as pltpu
from jax.sharding import PartitionSpec as P

MESH = pl.DeviceIdType.MESH
F32 = jnp.float32
BF16 = jnp.bfloat16

N = 4
EXPERTS = 3
D = 7168
FF = 2048
ROWS = 32
GROUP = N * N * ROWS
DEPTH = 56
CHUNK = 448
QUARTER = 1792
UNITS = 128
SPAN = 896

PLANE = (
    (1, 0), (3, 0), (0, 1), (0, 3), (2, 0), (0, 2), (1, 1), (3, 3),
    (2, 1), (1, 3), (3, 1), (2, 3), (1, 2), (3, 2), (2, 2),
)


def place():
    e = lax.axis_index("expert")
    t = lax.axis_index("tensor")
    y, xl, c = lax.div(e, 4), lax.rem(lax.div(e, 2), 2), lax.rem(e, 2)
    xh, z = lax.div(t, 4), lax.rem(t, 4)
    return e, t, y, xh * 2 + xl, z, c, xl, xh


def device(y, x, z, c):
    return {
        "expert": y * 4 + lax.rem(x, 2) * 2 + c,
        "tensor": lax.div(x, 2) * 4 + z,
    }


def ring(v, d):
    return lax.rem(v + d, N)


def kernel(
    tok, ids, scores, gate, up, down, out,
    xs, wg, wd, acc, hb, mask, total_ref, ob, back, order_ref, info,
    ssem, asend, arecv, wrecv, drecv, trecv, hrecv, irecv, osem, fsem, lsem,
):
    e_index, t_index, y, x, z, c, xl, xh = place()
    mine = e_index * 8 + t_index
    sends = []

    def send(src, dst, recv, to):
        cp = pltpu.make_async_remote_copy(
            src_ref=src,
            dst_ref=dst,
            send_sem=ssem.at[len(sends)],
            recv_sem=recv,
            device_id=to,
            device_id_type=MESH,
        )
        cp.start()
        sends.append(cp)

    def arrived(ref, sem):
        pltpu.make_async_copy(ref, ref, sem).wait()

    barrier = pltpu.get_barrier_semaphore()
    peers = [device(y, ring(x, dx), ring(z, dz), c) for dx, dz in PLANE]
    north, south = device(ring(y, 1), x, z, c), device(ring(y, 3), x, z, c)
    partner = device(y, x, z, 1 - c)
    for to in [*peers, north, south, partner]:
        pl.semaphore_signal(barrier, inc=1, device_id=to, device_id_type=MESH)

    marks = scores[...].astype(F32)
    info[xl, 0:2, :] = ids[...].astype(F32)
    info[xl, 2:4, :] = marks / (marks[0:1, :] + marks[1:2, :])

    own_rows = pl.ds(pl.multiple_of(mine * DEPTH, 8), DEPTH)
    before, after, across = ring(y, 3), ring(y, 1), ring(y, 2)

    def columns(px, pz):
        return pl.ds(pl.multiple_of((px * N + pz) * UNITS, UNITS), UNITS)

    own_tok = pltpu.make_async_copy(tok, xs.at[x, z], lsem)
    own_tok.start()
    for w in range(EXPERTS):
        for i, ref in enumerate((gate, up)):
            pltpu.make_async_copy(
                ref.at[w, :, columns(x, z)], wg.at[i, w, own_rows, :], arecv.at[min(w, 1), xl]
            ).start()

    def down_piece(w, cy, cc, cols=slice(None)):
        rows = pl.ds(pl.multiple_of(cc * DEPTH, 8), DEPTH)
        return wd.at[w, cy, rows, cols]

    own_down = []
    for w in range(EXPERTS):
        cp = pltpu.make_async_copy(down.at[w], down_piece(w, y, c), drecv.at[w, y, c])
        cp.start()
        own_down.append(cp)

    pl.semaphore_wait(barrier, len(peers) + 3)

    def down_own(w):
        for to in (north, south, partner):
            send(down.at[w], down_piece(w, y, c), drecv.at[w, y, c], to)

    def down_pass(w, cy, to, cols=slice(None)):
        ref = down_piece(w, cy, c, cols)
        send(ref, ref, drecv.at[w, cy, c], to)

    def down_wait(w, cy, cc):
        arrived(down_piece(w, cy, cc), drecv.at[w, cy, cc])

    def down_relay(w):
        down_wait(w, before, c)
        down_pass(w, before, north, slice(0, FF // 2))
        down_wait(w, after, c)
        down_pass(w, after, south, slice(FF // 2, FF))
        down_pass(w, before, partner)
        down_pass(w, after, partner)

    def down_far(w):
        down_wait(w, across, c)
        down_pass(w, across, partner)

    sets = (pl.ds(0, 1), pl.ds(1, EXPERTS - 1))

    def spread(k):
        for (dx, dz), to in zip(PLANE, peers):
            cols = columns(ring(x, dx), ring(z, dz))
            for i, ref in enumerate((gate, up)):
                pltpu.make_async_remote_copy(
                    src_ref=ref.at[sets[k], :, cols],
                    dst_ref=wg.at[i, sets[k], own_rows, :],
                    send_sem=asend.at[k],
                    recv_sem=arecv.at[k, xl],
                    device_id=to,
                    device_id_type=MESH,
                ).start()

    def chunk(w, cy, cx, cc):
        k = cy * 4 + cx * 2 + cc
        rows = pl.ds(pl.multiple_of(k * CHUNK, CHUNK), CHUNK)
        return wg.at[:, w, rows, :], wrecv.at[w, k]

    def pass_on(w, cy, cx, to):
        ref, sem = chunk(w, cy, cx, c)
        send(ref, ref, sem, to)

    def wait_chunk(w, cy, cx, cc):
        ref, sem = chunk(w, cy, cx, cc)
        arrived(ref, sem)

    def spread_here(k, cx):
        rows = pl.ds(pl.multiple_of((y * 4 + cx * 2 + c) * CHUNK, CHUNK), CHUNK)
        arrived(wg.at[:, sets[k], rows, :], arecv.at[k, cx])

    def own_chunks(w):
        if w < 2:
            spread_here(w, 0)
        pass_on(w, y, 0, north)
        if w < 2:
            spread_here(w, 1)
        pass_on(w, y, 1, south)
        pass_on(w, y, 1, north)
        pass_on(w, y, 0, south)
        pass_on(w, y, 0, partner)
        pass_on(w, y, 1, partner)

    def relay(w):
        wait_chunk(w, before, 0, c)
        pass_on(w, before, 0, north)
        wait_chunk(w, after, 1, c)
        pass_on(w, after, 1, south)
        pass_on(w, before, 0, partner)
        pass_on(w, after, 1, partner)

    def hand_over(w):
        wait_chunk(w, before, 1, c)
        pass_on(w, before, 1, partner)
        wait_chunk(w, after, 0, c)
        pass_on(w, after, 0, partner)

    def hand_over_far(w):
        for cx in range(2):
            wait_chunk(w, across, cx, c)
            pass_on(w, across, cx, partner)

    def from_partner(w, cy):
        for cx in range(2):
            wait_chunk(w, cy, cx, 1 - c)

    class Gather:
        def __init__(self, ref, sem, whole, low, high):
            self.ref, self.sem, self.whole, self.low, self.high = ref, sem, whole, low, high

        def block(self, half, a, b):
            return (ring(x, a), ring(z, b)) if half == 0 else (ring(x, b), ring(z, a))

        def to(self, half, leg, d):
            if (half + leg) % 2 == 0:
                return device(y, ring(x, d), z, c)
            return device(y, x, ring(z, d), c)

        def send(self, half, leg, a, b, d, part=None, src=None):
            bx, bz = self.block(half, a, b)
            part = (part or self.whole)[half]
            dst = self.ref.at[bx, bz, part[0], part[1]]
            src = dst if src is None else src.at[part[0], part[1]]
            send(src, dst, self.sem.at[half, bx, bz], self.to(half, leg, d))

        def wait(self, half, a, b):
            bx, bz = self.block(half, a, b)
            part = self.whole[half]
            arrived(self.ref.at[bx, bz, part[0], part[1]], self.sem.at[half, bx, bz])

        def start(self, src=None):
            for leg in range(2):
                for half in range(2):
                    for d in (1, 3):
                        self.send(half, leg, 0, 0, d, src=src)

        def near(self, a):
            for half in range(2):
                self.wait(half, a, 0)
                if a == 3:
                    self.send(half, 0, 3, 0, 1, self.low)
                elif a == 1:
                    self.send(half, 0, 1, 0, 3, self.high)
                self.send(half, 1, a, 0, 1)
                self.send(half, 1, a, 0, 3)

        def relay(self, a):
            for half in range(2):
                self.wait(half, a, 3)
                if a in (0, 3):
                    self.send(half, 1, a, 3, 1)
                self.wait(half, a, 1)
                if a in (1, 2):
                    self.send(half, 1, a, 1, 3)

        def far(self, a):
            for half in range(2):
                self.wait(half, a, 2)

    rows_all = pl.ds(0, ROWS)
    upper, lower = pl.ds(0, ROWS // 2), pl.ds(ROWS // 2, ROWS // 2)

    def token_gather(i):
        sides = [pl.ds((2 * i + j) * QUARTER, QUARTER) for j in range(2)]
        return Gather(
            xs, trecv.at[i],
            [(rows_all, s) for s in sides],
            [(upper, s) for s in sides],
            [(lower, s) for s in sides],
        )

    every = pl.ds(0, 2 * UNITS)

    def hidden_gather(i):
        part = lambda lo, n: pl.ds(i * GROUP // 2 + lo, n)
        return Gather(
            hb, hrecv.at[i],
            [(part(0, 128), every), (part(128, 128), every)],
            [(part(0, 64), every), (part(128, 64), every)],
            [(part(64, 64), every), (part(192, 64), every)],
        )

    tok_a, tok_b = token_gather(0), token_gather(1)
    hid_a, hid_b = hidden_gather(0), hidden_gather(1)

    down_own(0)
    spread(0)
    send(info.at[xl], info.at[xl], irecv, device(y, xh * 2 + 1 - xl, z, c))
    tok_a.start(tok)

    wd[:, :, 2 * DEPTH :, :] = jnp.zeros((EXPERTS, N, 128 - 2 * DEPTH, FF), BF16)
    lane = lax.broadcasted_iota(jnp.int32, (128, SPAN), 0)
    wanted = lax.broadcasted_iota(jnp.int32, (128, SPAN), 1)
    for q in range(8):
        spot = jnp.where(lane < DEPTH, lane, lane + CHUNK - DEPTH) + q * DEPTH
        spot = jnp.where(lane < 2 * DEPTH, spot, -1)
        order_ref[q * 128 : (q + 1) * 128, :] = jnp.where(spot == wanted, 1.0, 0.0).astype(BF16)

    arrived(info.at[1 - xl], irecv)
    route = []
    for bx in range(N):
        column = info[bx % 2][:, (bx // 2) * 128 : (bx // 2) * 128 + 128].T
        route.append(column)
        rows = slice(bx * N * ROWS, (bx + 1) * N * ROWS)
        for k in range(2):
            for w in range(EXPERTS):
                hit = jnp.where(column[:, k : k + 1] == float(w), 1.0, 0.0)
                mask[k, w, rows, :] = jnp.broadcast_to(hit, (N * ROWS, UNITS)).astype(BF16)

    def quarter(w, q):
        span = pl.ds(pl.multiple_of(q * QUARTER, 256), QUARTER)
        left = xs[:, :, :, span].reshape(GROUP, QUARTER)
        right = jnp.concatenate([wg[0, w, span, :], wg[1, w, span, :]], axis=1)
        acc[w] += jnp.dot(left, right, preferred_element_type=F32)

    def products(w, first):
        def one(q, carry):
            quarter(w, q)
            return carry

        lax.fori_loop(first, first + 2, one, 0)

    def all_from_partner(w):
        for cy in (y, before, after, across):
            from_partner(w, cy)

    def tokens_a_here():
        for a in range(N):
            tok_a.far(a)
        own_tok.wait()

    def tokens_b_here():
        for a in range(N):
            tok_b.far(a)

    acc[...] = jnp.zeros((EXPERTS, GROUP, 2 * UNITS), F32)
    own_chunks(0)
    spread(1)
    tok_a.near(3)
    tok_a.near(1)
    tok_b.start(tok)
    relay(0)
    own_chunks(1)
    tok_a.relay(0)
    tok_a.near(2)
    tok_a.relay(3)
    tok_a.relay(1)
    hand_over(0)
    relay(1)
    tok_b.near(3)
    tok_b.near(1)
    own_chunks(2)
    tok_a.relay(2)
    hand_over_far(0)
    tok_b.relay(0)
    tok_b.near(2)
    hand_over(1)
    tok_b.relay(3)
    tok_b.relay(1)
    relay(2)
    tokens_a_here()
    all_from_partner(0)
    products(0, 0)
    down_own(1)
    down_own(2)
    hand_over_far(1)
    tok_b.relay(2)
    all_from_partner(1)
    products(1, 0)
    tokens_b_here()
    def second_half(n, carry):
        quarter(lax.div(n, 2), 2 + lax.rem(n, 2))
        return carry

    lax.fori_loop(0, 4, second_half, 0)

    hand_over(2)
    hand_over_far(2)
    for cy in (y, before, after, across):
        from_partner(2, cy)
    def third(n, carry):
        quarter(2, n)
        return carry

    lax.fori_loop(0, 4, third, 0)

    for bx in range(N):
        rows = slice(bx * N * ROWS, (bx + 1) * N * ROWS)
        values = []
        for w in range(EXPERTS):
            g = acc[w, rows, 0:UNITS]
            u = acc[w, rows, UNITS : 2 * UNITS]
            values.append(g / (1.0 + jnp.exp(-g)) * u)
        column = info[bx % 2][:, (bx // 2) * 128 : (bx // 2) * 128 + 128].T
        for k in range(2):
            chosen = column[:, k : k + 1]
            value = jnp.where(chosen == 0.0, values[0], jnp.where(chosen == 1.0, values[1], values[2]))
            value = value * column[:, 2 + k : 3 + k]
            hb[x, z, rows, k * UNITS : (k + 1) * UNITS] = value.astype(BF16)

    near_blocks = [(a, b) for a in (0, 3, 1) for b in (0, 3, 1)]
    far_blocks = [(2, 0), (0, 2), (2, 3), (3, 2), (2, 1), (1, 2), (2, 2)]

    def down_products(i, blocks, start):
        rows = pl.ds(i * GROUP // 2, GROUP // 2)
        left, right = [], []
        for a, b in blocks:
            bx, bz = ring(x, a), ring(z, b)
            one, two = hb[bx, bz, rows, 0:UNITS], hb[bx, bz, rows, UNITS : 2 * UNITS]
            for w in range(EXPERTS):
                left.append(one * mask[0, w, rows, :] + two * mask[1, w, rows, :])
                right.append(wd[w, :, :, columns(bx, bz)].reshape(N * 128, UNITS))
        more = lax.dot_general(
            jnp.concatenate(left, axis=1), jnp.concatenate(right, axis=1),
            (((1,), (1,)), ((), ())), preferred_element_type=F32,
        )
        if start:
            total_ref[rows, :] = more
            return
        more = more + total_ref[rows, :]
        for cy in range(N):
            piece = more[:, cy * 128 : (cy + 1) * 128].astype(BF16)
            ob[2 * i : 2 * i + 2, :, cy, :, :] = piece.reshape(2, N, ROWS, 128)

    spot = back.at[xl, :, :, pl.ds(pl.multiple_of(t_index * 128, 128), 128)]

    def give_back(i):
        for near in (1, 0):
            bx = 2 * i + lax.rem(x + near, 2)
            for d in (1, 3, 2, 0):
                if near == 0 and d == 0:
                    continue
                bz = ring(z, d)
                send(ob.at[bx, bz], spot, osem, device(y, bx, bz, c))

        @pl.when(i == xh)
        def _():
            pltpu.make_async_copy(ob.at[x, z], spot, osem).start()

        @pl.when(i != xh)
        def _():
            pltpu.make_async_remote_copy(
                src_ref=ob.at[ring(x, 2), z],
                dst_ref=spot,
                send_sem=fsem,
                recv_sem=osem,
                device_id=device(y, ring(x, 2), z, c),
                device_id_type=MESH,
            ).start()

    hid_a.start()
    hid_b.start()
    hid_a.near(3)
    hid_a.near(1)
    down_relay(0)
    hid_a.relay(0)
    hid_a.near(2)
    hid_b.near(3)
    hid_b.near(1)
    down_relay(1)
    hid_a.relay(3)
    hid_a.relay(1)
    hid_b.relay(0)
    down_relay(2)
    hid_b.near(2)
    hid_a.relay(2)
    hid_b.relay(3)
    hid_b.relay(1)
    for w in range(EXPERTS):
        down_far(w)
    hid_b.relay(2)
    for w in range(EXPERTS):
        own_down[w].wait()
        for cy in (y, before, after, across):
            down_wait(w, cy, 1 - c)
    down_products(0, near_blocks, True)
    for a in range(N):
        hid_a.far(a)
    down_products(0, far_blocks, False)
    give_back(0)
    down_products(1, near_blocks, True)
    for a in range(N):
        hid_b.far(a)
    down_products(1, far_blocks, False)
    give_back(1)
    arrived(back, osem)
    result = jnp.dot(
        back[...].reshape(2 * N * ROWS, 8 * 128), order_ref[...], preferred_element_type=F32
    ).astype(BF16)
    for cx in range(2):
        for cy in range(N):
            k = cx * N + cy
            base = (cy * 2 + cx) * SPAN
            out[:, base : base + SPAN] = result[k * ROWS : (k + 1) * ROWS, :]

    for cp in sends:
        cp.wait_send()
    arrived(ob.at[ring(x, 2), z], fsem)
    for k in range(2):
        arrived(wg.at[:, sets[k], 0 : 15 * DEPTH, :], asend.at[k])


SENDS = 212


def local(tokens, expert_ids, gate_scores, gate_weight, up_weight, down_weight):
    any_space = pl.BlockSpec(memory_space=pl.ANY)
    vmem = pl.BlockSpec(memory_space=pltpu.VMEM)
    dma = pltpu.SemaphoreType.DMA
    return pl.pallas_call(
        kernel,
        out_shape=jax.ShapeDtypeStruct((ROWS, D), BF16),
        in_specs=[any_space, vmem, vmem, any_space, any_space, any_space],
        out_specs=vmem,
        scratch_shapes=[
            pltpu.VMEM((N, N, ROWS, D), BF16),
            pltpu.VMEM((2, EXPERTS, D, UNITS), BF16),
            pltpu.VMEM((EXPERTS, N, 128, FF), BF16),
            pltpu.VMEM((EXPERTS, GROUP, 2 * UNITS), F32),
            pltpu.VMEM((N, N, GROUP, 2 * UNITS), BF16),
            pltpu.VMEM((2, EXPERTS, GROUP, UNITS), BF16),
            pltpu.VMEM((GROUP, N * 128), F32),
            pltpu.VMEM((N, N, N, ROWS, 128), BF16),
            pltpu.VMEM((2, N, ROWS, 8 * 128), BF16),
            pltpu.VMEM((8 * 128, SPAN), BF16),
            pltpu.VMEM((2, 8, 256), F32),
            dma((SENDS,)),
            dma((2,)),
            dma((2, 2)),
            dma((EXPERTS, 16)),
            dma((EXPERTS, N, 2)),
            dma((2, 2, N, N)),
            dma((2, 2, N, N)),
            dma,
            dma,
            dma,
            dma,
        ],
        compiler_params=pltpu.CompilerParams(
            collective_id=0, has_side_effects=True, vmem_limit_bytes=64000 * 1024
        ),
        name="relay_experts",
    )(tokens, expert_ids.T, gate_scores.T, gate_weight, up_weight, down_weight)


def solution(mesh):
    return jax.shard_map(
        local,
        mesh=mesh,
        in_specs=(
            P(("expert", "tensor"), None),
            P("expert", None),
            P("expert", None),
            P(None, ("expert", "tensor"), None),
            P(None, ("expert", "tensor"), None),
            P(None, ("expert", "tensor"), None),
        ),
        out_specs=P(("expert", "tensor"), None),
        check_vma=False,
    )
```
